128 devices in a mesh: req: 32 (over x, z, core), head: 4 (over y).
Axes of the slice: x: 4, y: 4, z: 4, core: 2. Of those that a mesh axis runs over, the one named last changes fastest.
Arguments:
- streams: bfloat16 [128, 64, 4, 2048], P('req'), may hold values from -6 to 6
- w_query: bfloat16 [2048, 2048], P(None, 'head'), may hold values from -0.125 to 0.125
- w_key: bfloat16 [2048, 2048], P(None, 'head'), may hold values from -0.125 to 0.125
- w_value: bfloat16 [2048, 2048], P(None, 'head'), may hold values from -0.125 to 0.125
- w_output: bfloat16 [2048, 2048], P('head'), may hold values from -0.125 to 0.125
- w_gate: bfloat16 [2048, 8192], P(None, 'req'), may hold values from -0.125 to 0.125
- w_up: bfloat16 [2048, 8192], P(None, 'req'), may hold values from -0.125 to 0.125
- w_down: bfloat16 [8192, 2048], P('req'), may hold values from -0.0625 to 0.0625
- cache_keys: bfloat16 [128, 1024, 2048], P('req', None, 'head'), may hold values from -250 to 250
- cache_values: bfloat16 [128, 1024, 2048], P('req', None, 'head'), may hold values from -6 to 6
- hc_in: float32 [2, 4], replicated, may hold values from 0.1 to 0.6
- hc_res: float32 [2, 4, 4], replicated, may hold values from -0.4 to 0.8
- hc_out: float32 [2, 4], replicated, may hold values from 0.5 to 1.5
- parents: int32 [128, 64], replicated, may hold values from 0 to 62, as said below
- draft_len: int32 [128], replicated, may hold values from 1 to 64, 6144 in all
- cache_len: int32 [128], replicated, may hold values from 1 to 1024, 65536 in all
- accept_pick: int32 [128], replicated, may hold values from 0 to 63
- slot_owner: int32 [128], replicated, may hold values from 0 to 127, each once
Outputs:
- new_streams: bfloat16 [128, 64, 4, 2048], P('req', 'head')
- accepted_kv: bfloat16 [128, 64, 2, 2048], P('req', None, None, 'head')
The draws below stay inside these ranges and needn't reach their ends.
Inputs may be any that keep to these rules, and one draw needn't show every extreme that they name: parents[r, 0] = 0 and 0 <= parents[r, p] < p for p >= 1. `draft_len`: the live draft nodes of all requests sum to exactly 6144.
All inputs are finite; a program needn't handle non-finite values.
Results may differ from the reference program's by a relative error of at most 0.024.
Values may be sent and summed in bfloat16 or wider, within the bound.
No kernel may reach another device: no remote copies, remote signals or barrier semaphores. Data moves between devices by JAX's collectives and lax.ppermute only.
A program may use at most 128 MiB of HBM per device.

```python
import math
import jax
import jax.numpy as jnp
import numpy as np
from jax import lax

D = 2048
HEADS = 16
HD = 128
FF = 8192
NS = 4
DRAFT = 64
CACHE = 1024
REQS = 128
VALID = 6144


def draw_parents(key, part):
    nodes = jnp.arange(DRAFT, dtype=jnp.int32)
    reach = jnp.maximum(jnp.minimum(nodes, 4), 1)
    offset = jax.random.randint(key, (REQS, DRAFT), 0, 1 << 20, dtype=jnp.int32) % reach[None, :]
    chosen = jnp.where(nodes[None, :] == 0, 0, nodes[None, :] - 1 - offset)
    chosen = jnp.where(nodes[None, :] == DRAFT - 1, DRAFT - 2, chosen)
    return jnp.maximum(chosen, 0).astype(jnp.int32)


def draw_cache_keys(key, part):
    base = jax.random.truncated_normal(key, -5.0, 5.0, (REQS, CACHE, HEADS * HD), jnp.float32)
    return base.astype(jnp.bfloat16)


def place_ends(entries, stream_key, least, largest):
    place = [jax.random.randint(jax.random.fold_in(stream_key, axis), (), 0, length) for axis, length in enumerate(entries.shape)]
    main_axis = entries.shape.index(max(entries.shape))
    next_to = place[:main_axis] + [(place[main_axis] + 1) % entries.shape[main_axis]] + place[main_axis + 1:]
    return entries.at[tuple(place)].set(least).at[tuple(next_to)].set(largest)


def block_levels(rng, dims, cuts, least, largest):
    factor_of = 1.0
    for dim, blocks in cuts:
        draws = jax.random.uniform(jax.random.fold_in(jax.random.fold_in(rng, 6), dim), (blocks,), jnp.float32, least / len(cuts), largest / len(cuts))
        factor_of = factor_of * jnp.repeat(jnp.exp(draws), dims[dim] // blocks).reshape((-1,) + (1,) * (len(dims) - 1 - dim))
    return factor_of


def length_profile(number_of, total, most, skew):
    loads = [(1 << 20) // math.isqrt(standing ** skew) + 1 for standing in range(2, number_of + 1)]
    spare, given = total - most - (number_of - 1), [1] * (number_of - 1)
    while spare > 0:
        candidates = [i for i in range(number_of - 1) if given[i] < most]
        pool, budget = sum([loads[i] for i in candidates]), spare
        for i in candidates:
            addition = min(most - given[i], max(1, budget * loads[i] // pool), spare)
            given[i] = given[i] + addition
            spare = spare - addition
    return np.array([most] + given)


def ragged_sizes(own_key, number_of, total, bound, lean):
    if number_of == 2:
        one = jax.random.randint(own_key, (), max(1, total - bound), min(bound, total - 1) + 1)
        return jnp.stack([one, total - one])
    tallies = jnp.asarray(length_profile(number_of, total, bound, lean), jnp.int32)
    couples = (number_of - 1) // 2
    donor, receiver = tallies[1:1 + 2 * couples:2], tallies[2:2 + 2 * couples:2]
    margin = jnp.minimum(donor - 1, bound - receiver)
    passed = jax.random.randint(jax.random.fold_in(own_key, 1), (couples,), 0, 1 << 20) % (margin + 1)
    tallies = tallies.at[1:1 + 2 * couples:2].set(donor - passed).at[2:2 + 2 * couples:2].set(receiver + passed)
    return tallies[jax.random.permutation(jax.random.fold_in(own_key, 2), number_of)]


def scatter_about(key, dims, deviation, most, pieces=(), held_as=jnp.bfloat16):
    values = deviation * jax.random.normal(key, dims, jnp.float32)
    if pieces:
        values = values * block_levels(key, dims, pieces, -0.22, 0.18)
    return jnp.clip(values, -most, most).astype(held_as)


def setup_inputs(seed: int = 0) -> dict:
    streams_of = jax.random.split(jax.random.key(seed), 19)
    return {
        "streams": scatter_about(streams_of[0], (REQS, DRAFT, NS, D), 1.0, 6.0, ((0, 32),)),
        "w_query": scatter_about(streams_of[1], (D, HEADS * HD), D ** -0.5, 0.125, ((1, 4),)),
        "w_key": scatter_about(streams_of[2], (D, HEADS * HD), D ** -0.5, 0.125, ((1, 4),)),
        "w_value": scatter_about(streams_of[3], (D, HEADS * HD), D ** -0.5, 0.125, ((1, 4),)),
        "w_output": scatter_about(streams_of[4], (HEADS * HD, D), (HEADS * HD) ** -0.5, 0.125, ((0, 4),)),
        "w_gate": scatter_about(streams_of[5], (D, FF), D ** -0.5, 0.125, ((1, 32),)),
        "w_up": scatter_about(streams_of[6], (D, FF), D ** -0.5, 0.125, ((1, 32),)),
        "w_down": scatter_about(streams_of[7], (FF, D), FF ** -0.5, 0.0625, ((0, 32),)),
        "cache_keys": draw_cache_keys(jax.random.fold_in(streams_of[18], 71), 0),
        "cache_values": scatter_about(streams_of[9], (REQS, CACHE, HEADS * HD), 1.0, 6.0, ((0, 32), (2, 4))),
        "hc_in": jnp.clip(jax.random.uniform(streams_of[10], (2, NS), jnp.float32, 0.1, 0.6), 0.1, 0.6),
        "hc_res": jnp.clip(jax.random.uniform(streams_of[11], (2, NS, NS), jnp.float32, -0.4, 0.8), -0.4, 0.8),
        "hc_out": jnp.clip(jax.random.uniform(streams_of[12], (2, NS), jnp.float32, 0.5, 1.5), 0.5, 1.5),
        "parents": draw_parents(jax.random.fold_in(streams_of[18], 71), 0),
        "draft_len": ragged_sizes(streams_of[14], REQS, VALID, DRAFT, 1).astype(jnp.int32),
        "cache_len": ragged_sizes(streams_of[15], REQS, REQS * CACHE // 2, CACHE, 2).astype(jnp.int32),
        "accept_pick": place_ends(jax.random.randint(streams_of[16], (REQS,), 0, DRAFT), jax.random.fold_in(streams_of[16], 1), 0, DRAFT - 1).astype(jnp.int32),
        "slot_owner": jax.random.permutation(streams_of[17], REQS).astype(jnp.int32),
    }


def ancestry(parent_ids):
    count = parent_ids.shape[-1]
    nodes = jnp.arange(count, dtype=jnp.int32)
    links = (parent_ids[..., :, None] == nodes).astype(jnp.float32)
    unit = (nodes[:, None] == nodes[None, :]).astype(jnp.float32)
    above = jnp.minimum(links + unit, 1.0)
    for rounds in range((count - 1).bit_length()):
        above = jnp.minimum(jnp.matmul(above, above, precision=lax.Precision.HIGHEST), 1.0)
    depth = lax.optimization_barrier(jnp.sum(above, axis=-1)) - 1.0
    return (above, depth)

def normalize(values):
    center = lax.optimization_barrier(jnp.mean(values, axis=-1, keepdims=True))
    spread = lax.optimization_barrier(jnp.mean(jnp.square(values - center), axis=-1, keepdims=True))
    return (values - center) * lax.rsqrt(spread + 1e-05)

def rotate(values, position, head_size):
    half = head_size // 2
    freq = jnp.power(10000.0, -(jnp.arange(half, dtype=jnp.float32) * 2.0 / head_size))
    angle = position[..., None] * freq
    shaped = values.reshape(values.shape[:-1] + (-1, head_size))
    first, second = (shaped[..., :half], shaped[..., half:])
    cosine = jnp.cos(angle)[..., None, :]
    sine = jnp.sin(angle)[..., None, :]
    turned = jnp.concatenate([first * cosine - second * sine, second * cosine + first * sine], axis=-1)
    return turned.reshape(values.shape)

def reference(streams, w_query, w_key, w_value, w_output, w_gate, w_up, w_down, cache_keys, cache_values, hc_in, hc_res, hc_out, parents, draft_len, cache_len, accept_pick, slot_owner):
    highest = lax.Precision.HIGHEST
    scale = HD ** (-0.5)

    def per_slot(slot):
        owner = slot_owner[slot]
        parent_ids = parents[owner]
        draft_count = draft_len[owner]
        cache_count = cache_len[owner]
        accepted = jnp.minimum(accept_pick[owner], draft_count - 1)
        above, depth = ancestry(parent_ids)
        nodes = jnp.arange(DRAFT, dtype=jnp.int32)
        hidden = streams[slot].astype(jnp.float32)
        mixed_in = jnp.einsum('pmd,m->pd', hidden, hc_in[0], precision=highest)
        normed = normalize(mixed_in).astype(jnp.bfloat16)
        position = cache_count.astype(jnp.float32) + depth
        query = rotate(jnp.dot(normed, w_query, preferred_element_type=jnp.float32), position, HD).astype(jnp.bfloat16)
        keys = rotate(jnp.dot(normed, w_key, preferred_element_type=jnp.float32), position, HD).astype(jnp.bfloat16)
        values = jnp.dot(normed, w_value, preferred_element_type=jnp.float32).astype(jnp.bfloat16)
        query_h = query.reshape(DRAFT, HEADS, HD).astype(jnp.float32)
        keys_h = keys.reshape(DRAFT, HEADS, HD).astype(jnp.float32)
        values_h = values.reshape(DRAFT, HEADS, HD).astype(jnp.float32)
        stored_keys = cache_keys[slot].reshape(CACHE, HEADS, HD).astype(jnp.float32)
        stored_values = cache_values[slot].reshape(CACHE, HEADS, HD).astype(jnp.float32)
        cached = jnp.einsum('phe,che->hpc', query_h, stored_keys) * scale
        live = jnp.arange(CACHE, dtype=jnp.int32) < cache_count
        cached = jnp.where(live[None, None, :], cached, -1e+30)
        local = jnp.einsum('phe,qhe->hpq', query_h, keys_h) * scale
        local = jnp.where((above > 0.5)[None, :, :], local, -1e+30)
        top = jnp.maximum(lax.optimization_barrier(jnp.max(cached, axis=-1)), lax.optimization_barrier(jnp.max(local, axis=-1)))[..., None]
        cached_exp = jnp.exp(cached - top)
        local_exp = jnp.exp(local - top)
        total = lax.optimization_barrier(jnp.sum(cached_exp, axis=-1, keepdims=True)) + lax.optimization_barrier(jnp.sum(local_exp, axis=-1, keepdims=True))
        weight_cache = (cached_exp / total).astype(jnp.bfloat16).astype(jnp.float32)
        weight_local = (local_exp / total).astype(jnp.bfloat16).astype(jnp.float32)
        attended = jnp.einsum('hpc,che->phe', weight_cache, stored_values) + jnp.einsum('hpq,qhe->phe', weight_local, values_h)
        attended = attended.astype(jnp.bfloat16).reshape(DRAFT, HEADS * HD)
        attn_out = jnp.dot(attended, w_output, preferred_element_type=jnp.float32)
        carried = jnp.einsum('pnd,nm->pmd', hidden, hc_res[0], precision=highest) + hc_out[0][None, :, None] * attn_out[:, None, :]
        first = carried.astype(jnp.bfloat16).astype(jnp.float32)
        mlp_in = normalize(jnp.einsum('pmd,m->pd', first, hc_in[1], precision=highest)).astype(jnp.bfloat16)
        gate = jnp.dot(mlp_in, w_gate, preferred_element_type=jnp.float32)
        upward = jnp.dot(mlp_in, w_up, preferred_element_type=jnp.float32)
        inner = (jax.nn.silu(gate) * upward).astype(jnp.bfloat16)
        mlp_out = jnp.dot(inner, w_down, preferred_element_type=jnp.float32)
        final = jnp.einsum('pnd,nm->pmd', first, hc_res[1], precision=highest) + hc_out[1][None, :, None] * mlp_out[:, None, :]
        valid = nodes < draft_count
        final = jnp.where(valid[:, None, None], final, 0.0).astype(jnp.bfloat16)
        path_row = lax.optimization_barrier(jnp.sum(jnp.where((nodes == accepted)[:, None], above, 0.0), axis=0))
        take = ((depth[None, :] == nodes[:, None].astype(jnp.float32)) & (path_row[None, :] > 0.5)).astype(jnp.bfloat16)
        new_keys = jnp.dot(take, keys, preferred_element_type=jnp.float32).astype(jnp.bfloat16)
        new_values = jnp.dot(take, values, preferred_element_type=jnp.float32).astype(jnp.bfloat16)
        kept = jnp.stack([new_keys, new_values], axis=1)
        return (final, kept)
    outputs = lax.map(per_slot, jnp.arange(REQS, dtype=jnp.int32))
    return (outputs[0], outputs[1])
```

```python
import functools

import jax
import jax.numpy as jnp
import numpy as np
from jax import lax
from jax.experimental import pallas as pl
from jax.experimental.pallas import tpu as pltpu
from jax.sharding import PartitionSpec as P

HD = 128
SLOTS = 4
DRAFT = 64
CACHE = 1024
D = 2048
NS = 4
LT = D // 128
Q = 16
SCALE = HD ** (-0.5)
BF = jnp.bfloat16
F32 = jnp.float32
NT = (((1,), (1,)), ((), ()))


def mm(a, b):
    return jnp.dot(a, b, preferred_element_type=F32)


def mm_nt(a, b):
    return lax.dot_general(a, b, NT, preferred_element_type=F32)


def normalize(x):
    center = jnp.sum(x, axis=-1, keepdims=True) * (1.0 / D)
    y = x - center
    spread = jnp.sum(y * y, axis=-1, keepdims=True) * (1.0 / D)
    return y * lax.rsqrt(spread + 1e-05)


def front_kernel(
    place,
    owner,
    dlen,
    clen,
    pick,
    hc_in,
    parents,
    freq,
    st,
    wq,
    wk,
    wv,
    ck,
    cv,
    wo,
    out,
    kv_out,
    raw,
    xbuf,
    normed,
    above_s,
    take_s,
    cos_s,
    sin_s,
    att,
    acc,
    kvs,
):
    i = pl.program_id(0)
    base = place[0] * SLOTS

    @pl.when(i < SLOTS)
    def _():
        s = i
        r = owner[base + s]
        raw[...] = st[...].astype(F32)
        rows = DRAFT
        for j in range(LT):
            x = hc_in[0, 0] * raw[pl.ds(j * NS, rows, stride=LT * NS), :]
            for m in range(1, NS):
                x = x + hc_in[0, m] * raw[pl.ds(j * NS + m, rows, stride=LT * NS), :]
            xbuf[:, j * 128 : (j + 1) * 128] = x
        normed[pl.ds(pl.multiple_of(s * DRAFT, DRAFT), DRAFT), :] = normalize(xbuf[...]).astype(BF)
        par = parents[pl.ds(r, 1), :]
        qi = lax.broadcasted_iota(jnp.int32, (DRAFT, DRAFT), 0)
        pi = lax.broadcasted_iota(jnp.int32, (DRAFT, DRAFT), 1)
        eye = (qi == pi).astype(F32)
        up = jnp.where(par == qi, 1.0, eye)
        for rounds in range(6):
            b = up.astype(BF)
            up = jnp.minimum(mm(b, b), 1.0)
        above = mm_nt(eye.astype(BF), up.astype(BF))
        above_s[s] = above
        depth_row = jnp.sum(up, axis=0, keepdims=True) - 1.0
        depth = jnp.sum(above, axis=1, keepdims=True) - 1.0
        a = jnp.minimum(pick[r], dlen[r] - 1)
        path = above_s[s, pl.ds(a, 1), :]
        take = jnp.where(depth_row == qi.astype(F32), path, 0.0)
        take_s[s] = take.astype(BF)
        angle = (clen[r].astype(F32) + depth) * freq[...]
        lane = lax.broadcasted_iota(jnp.int32, (DRAFT, HD), 1)
        at = pl.ds(pl.multiple_of(s * DRAFT, DRAFT), DRAFT)
        cos_s[at, :] = jnp.cos(angle)
        sine = jnp.sin(angle)
        sin_s[at, :] = jnp.where(lane < HD // 2, -sine, sine)

    @pl.when(i >= SLOTS)
    def _():
        g = i - SLOTS
        x = normed[...]
        q2 = mm(x, wq[...])
        k2 = mm(x, wk[...])
        v2 = mm(x, wv[...]).astype(BF)
        cosine = cos_s[...]
        sine = sin_s[...]
        col = lax.broadcasted_iota(jnp.int32, (DRAFT, CACHE), 1)
        for hh in range(2):
            cols = slice(hh * HD, (hh + 1) * HD)
            qh = q2[:, cols]
            kh = k2[:, cols]
            qh = (qh * cosine + pltpu.roll(qh, HD // 2, 1) * sine).astype(BF)
            kh = (kh * cosine + pltpu.roll(kh, HD // 2, 1) * sine).astype(BF)
            vh = v2[:, cols]
            for s in range(SLOTS):
                at = slice(s * DRAFT, (s + 1) * DRAFT)
                length = clen[owner[base + s]]
                qs, ks, vs = qh[at], kh[at], vh[at]
                sc = mm_nt(qs, ck[s, :, cols]) * SCALE
                sc = jnp.where(col < length, sc, -1e30)
                lo = mm_nt(qs, ks) * SCALE
                lo = jnp.where(above_s[s] > 0.5, lo, -1e30)
                top = jnp.maximum(
                    jnp.max(sc, axis=-1, keepdims=True), jnp.max(lo, axis=-1, keepdims=True)
                )
                e1 = jnp.exp(sc - top)
                e2 = jnp.exp(lo - top)
                total = jnp.sum(e1, axis=-1, keepdims=True) + jnp.sum(e2, axis=-1, keepdims=True)
                inv = 1.0 / total
                w1 = (e1 * inv).astype(BF)
                w2 = (e2 * inv).astype(BF)
                o = mm(w1, cv[s, :, cols]) + mm(w2, vs)
                att[at, cols] = o.astype(BF)
                tk = take_s[s]
                kvs[s, pl.ds((g * 2 + hh) * 2, DRAFT, stride=8), :] = mm(tk, ks)
                kvs[s, pl.ds((g * 2 + hh) * 2 + 1, DRAFT, stride=8), :] = mm(tk, vs)
        part = mm(att[...], wo[...])

        @pl.when(g == 0)
        def _():
            acc[...] = part

        @pl.when(g == 1)
        def _():
            full = (acc[...] + part).astype(BF)
            for s in range(SLOTS):
                for y in range(4):
                    out[y, s * Q : (s + 1) * Q, :] = full[
                        s * DRAFT + y * Q : s * DRAFT + (y + 1) * Q
                    ]
                kv_out[s * 512 : (s + 1) * 512, :] = kvs[s].astype(BF)


def front(place, owner, dlen, clen, pick, hc_in, parents, freq, st, wq, wk, wv, ck, cv, wo):
    smem = pl.BlockSpec(memory_space=pltpu.SMEM)
    head = lambda i, *_: (0, jnp.maximum(i - SLOTS, 0))
    cache = lambda i, *_: (0, 0, jnp.maximum(i - SLOTS, 0))
    return pl.pallas_call(
        front_kernel,
        name="front",
        out_shape=(
            jax.ShapeDtypeStruct((4, SLOTS * Q, D), BF),
            jax.ShapeDtypeStruct((2048, 128), BF),
        ),
        grid_spec=pltpu.PrefetchScalarGridSpec(
            num_scalar_prefetch=5,
            grid=(SLOTS + 2,),
            in_specs=[
                smem,
                pl.BlockSpec((128, DRAFT), lambda i, *_: (0, 0)),
                pl.BlockSpec((1, HD), lambda i, *_: (0, 0)),
                pl.BlockSpec((4096, 128), lambda i, *_: (jnp.minimum(i, SLOTS - 1), 0)),
                pl.BlockSpec((D, 256), head),
                pl.BlockSpec((D, 256), head),
                pl.BlockSpec((D, 256), head),
                pl.BlockSpec((SLOTS, CACHE, 256), cache),
                pl.BlockSpec((SLOTS, CACHE, 256), cache),
                pl.BlockSpec((256, D), lambda i, *_: (jnp.maximum(i - SLOTS, 0), 0)),
            ],
            out_specs=[
                pl.BlockSpec((4, SLOTS * Q, D), lambda i, *_: (0, 0, 0)),
                pl.BlockSpec((2048, 128), lambda i, *_: (0, 0)),
            ],
            scratch_shapes=[
                pltpu.VMEM((4096, 128), F32),
                pltpu.VMEM((DRAFT, D), F32),
                pltpu.VMEM((SLOTS * DRAFT, D), BF),
                pltpu.VMEM((SLOTS, DRAFT, DRAFT), F32),
                pltpu.VMEM((SLOTS, DRAFT, DRAFT), BF),
                pltpu.VMEM((SLOTS * DRAFT, HD), F32),
                pltpu.VMEM((SLOTS * DRAFT, HD), F32),
                pltpu.VMEM((SLOTS * DRAFT, 256), BF),
                pltpu.VMEM((SLOTS * DRAFT, D), F32),
                pltpu.VMEM((SLOTS, 512, 128), F32),
            ],
        ),
        compiler_params=pltpu.CompilerParams(vmem_limit_bytes=56 * 2**20),
    )(place, owner, dlen, clen, pick, hc_in, parents, freq, st, wq, wk, wv, ck, cv, wo)


def mid_kernel(place, hc_in, hc_res, hc_out, parts, st, first, rows_a, rows_b, raw, xbuf):
    i = pl.program_id(0)
    raw[...] = st[...].astype(F32)
    for j in range(LT):
        lanes = slice(j * 128, (j + 1) * 128)
        attn = parts[0, :, lanes].astype(F32)
        for y in range(1, 4):
            attn = attn + parts[y, :, lanes].astype(F32)
        own = [raw[pl.ds(j * NS + n, Q, stride=LT * NS), :] for n in range(NS)]
        x = None
        for m in range(NS):
            c = hc_out[0, m] * attn
            for n in range(NS):
                c = c + hc_res[0, n, m] * own[n]
            c = c.astype(BF)
            first[m, :, lanes] = c
            t = hc_in[1, m] * c.astype(F32)
            x = t if x is None else x + t
        xbuf[:, lanes] = x
    normed = normalize(xbuf[...]).astype(BF)

    @pl.when(i < 2)
    def _():
        rows_a[...] = normed

    @pl.when(i >= 2)
    def _():
        rows_b[...] = normed


def mid(place, hc_in, hc_res, hc_out, parts, st):
    smem = pl.BlockSpec(memory_space=pltpu.SMEM)
    half = SLOTS * Q // 2
    return pl.pallas_call(
        mid_kernel,
        name="mid",
        out_shape=(
            jax.ShapeDtypeStruct((NS, SLOTS * Q, D), BF),
            jax.ShapeDtypeStruct((half, D), BF),
            jax.ShapeDtypeStruct((half, D), BF),
        ),
        grid_spec=pltpu.PrefetchScalarGridSpec(
            num_scalar_prefetch=1,
            grid=(SLOTS,),
            in_specs=[
                smem,
                smem,
                smem,
                pl.BlockSpec((4, Q, D), lambda i, p: (0, i, 0)),
                pl.BlockSpec((1024, 128), lambda i, p: (i * 4 + p[1], 0)),
            ],
            out_specs=[
                pl.BlockSpec((NS, Q, D), lambda i, p: (0, i, 0)),
                pl.BlockSpec((Q, D), lambda i, p: (jnp.minimum(i, 1), 0)),
                pl.BlockSpec((Q, D), lambda i, p: (jnp.maximum(i - 2, 0), 0)),
            ],
            scratch_shapes=[pltpu.VMEM((1024, 128), F32), pltpu.VMEM((Q, D), F32)],
        ),
    )(place, hc_in, hc_res, hc_out, parts, st)


def last_kernel(place, owner, dlen, hc_res, hc_out, first, *refs):
    parts_a, parts_b, out, raw, mlp_s = refs[:4], refs[4:8], refs[8], refs[9], refs[10]
    i = pl.program_id(0)

    @pl.when(i < 2)
    def _():
        t = parts_a[0][...].astype(F32)
        for p in parts_a[1:]:
            t = t + p[...].astype(F32)
        mlp_s[...] = t

    @pl.when(i >= 2)
    def _():
        t = parts_b[0][...].astype(F32)
        for p in parts_b[1:]:
            t = t + p[...].astype(F32)
        mlp_s[...] = t

    count = dlen[owner[place[0] * SLOTS + i]]
    spot = place[1] * Q + lax.broadcasted_iota(jnp.int32, (Q, 128), 0)
    alive = spot < count
    for j in range(LT):
        lanes = slice(j * 128, (j + 1) * 128)
        mlp = mlp_s[:, lanes]
        f = [first[n, :, lanes].astype(F32) for n in range(NS)]
        for m in range(NS):
            c = hc_out[1, m] * mlp
            for n in range(NS):
                c = c + hc_res[1, n, m] * f[n]
            raw[pl.ds(j * NS + m, Q, stride=LT * NS), :] = jnp.where(alive, c, 0.0)
    out[...] = raw[...].astype(BF)


def last(place, owner, dlen, hc_res, hc_out, first, parts_a, parts_b):
    smem = pl.BlockSpec(memory_space=pltpu.SMEM)
    a_spec = pl.BlockSpec((Q, D), lambda i, *_: (jnp.minimum(i, 1), 0))
    b_spec = pl.BlockSpec((Q, D), lambda i, *_: (jnp.maximum(i - 2, 0), 0))
    return pl.pallas_call(
        last_kernel,
        name="last",
        out_shape=jax.ShapeDtypeStruct((SLOTS * 1024, 128), BF),
        grid_spec=pltpu.PrefetchScalarGridSpec(
            num_scalar_prefetch=3,
            grid=(SLOTS,),
            in_specs=[smem, smem, pl.BlockSpec((NS, Q, D), lambda i, *_: (0, i, 0))]
            + [a_spec] * 4
            + [b_spec] * 4,
            out_specs=pl.BlockSpec((1024, 128), lambda i, *_: (i, 0)),
            scratch_shapes=[pltpu.VMEM((1024, 128), F32), pltpu.VMEM((Q, D), F32)],
        ),
    )(place, owner, dlen, hc_res, hc_out, first, *parts_a, *parts_b)


def ffn_kernel(sizes, outs, *refs):
    n = len(sizes)
    xs, (g0, g1, u0, u1, d0, d1) = refs[:n], refs[n : n + 6]
    ys, cat = refs[n + 6 : -1], refs[-1]
    o = 0
    for x, size in zip(xs, sizes):
        cat[o : o + size, :] = x[...]
        o += size
    step = 256
    done = 0
    where = 0
    for c in range(o // step):
        x = cat[c * step : (c + 1) * step, :]
        total = None
        for g, u, d in ((g0, u0, d0), (g1, u1, d1)):
            gate = mm(x, g[...])
            inner = (gate / (1.0 + jnp.exp(-gate)) * mm(x, u[...])).astype(BF)
            t = mm(inner, d[...])
            total = t if total is None else total + t
        total = total.astype(BF)
        pos = 0
        while pos < step:
            size = outs[where]
            ys[where][...] = total[pos : pos + size]
            pos += size
            where += 1


def ffn(xs, weights, outs):
    sizes = tuple(x.shape[0] for x in xs)
    vmem = pl.BlockSpec(memory_space=pltpu.VMEM)
    rows = sum(sizes)
    return pl.pallas_call(
        functools.partial(ffn_kernel, sizes, outs),
        name="ffn",
        out_shape=tuple(jax.ShapeDtypeStruct((o, D), BF) for o in outs),
        in_specs=[vmem] * (len(xs) + 6),
        out_specs=tuple([vmem] * len(outs)),
        scratch_shapes=[pltpu.VMEM((rows, D), BF)],
        cost_estimate=pl.CostEstimate(
            flops=rows * D * 512 * 6, transcendentals=rows * 512, bytes_accessed=rows * D * 4
        ),
        compiler_params=pltpu.CompilerParams(vmem_limit_bytes=56 * 2**20),
    )(*xs, *weights)


def shift_pairs(axis, step):
    pairs = []
    for x in range(4):
        for z in range(4):
            for c in range(2):
                tx = (x + step) % 4 if axis == "x" else x
                tz = (z + step) % 4 if axis == "z" else z
                pairs.append((x * 8 + z * 2 + c, tx * 8 + tz * 2 + c))
    return pairs


def shift(v, axis, step):
    return lax.ppermute(v, "req", shift_pairs(axis, step))


def swap_core(v):
    return lax.ppermute(v, "req", [(i, i ^ 1) for i in range(32)])


def add(a, b):
    return (a.astype(F32) + b.astype(F32)).astype(BF)


def body(
    streams,
    w_query,
    w_key,
    w_value,
    w_output,
    w_gate,
    w_up,
    w_down,
    cache_keys,
    cache_values,
    hc_in,
    hc_res,
    hc_out,
    parents,
    draft_len,
    cache_len,
    accept_pick,
    slot_owner,
):
    place = jnp.stack([lax.axis_index("req"), lax.axis_index("head")]).astype(jnp.int32)
    half = np.arange(64, dtype=np.float64)
    freq = np.power(10000.0, -(half * 2.0 / HD)).astype(np.float32)
    freq = jnp.asarray(np.concatenate([freq, freq])[None, :])
    st = streams.reshape(SLOTS, DRAFT, NS, LT, 128).transpose(0, 1, 3, 2, 4).reshape(-1, 128)
    weights = (w_gate, swap_core(w_gate), w_up, swap_core(w_up), w_down, swap_core(w_down))
    part, kv = front(
        place,
        slot_owner,
        draft_len,
        cache_len,
        accept_pick,
        hc_in,
        parents,
        freq,
        st,
        w_query,
        w_key,
        w_value,
        cache_keys,
        cache_values,
        w_output,
    )
    parts = lax.all_to_all(part, "head", 0, 0, tiled=False)
    first, rows_a, rows_b = mid(place, hc_in, hc_res, hc_out, parts, st)

    order = (("x", "z", rows_a), ("z", "x", rows_b))
    own4 = []
    for one, two, rows in order:
        own4.append(
            jnp.concatenate(
                [rows, shift(rows, one, 1), shift(rows, one, -1), shift(rows, one, 2)], axis=0
            )
        )
    near = []
    for (one, two, _), x in zip(order, own4):
        near.append((shift(x, two, 1), shift(x, two, -1)))
    far = []
    for (one, two, _), (l, r) in zip(order, near):
        far.append((shift(l[:64], two, 1), shift(r[64:], two, -1)))

    own_out = ffn(own4, weights, (128, 128))
    near_out = ffn([near[0][0], near[0][1], near[1][0], near[1][1]], weights, (64,) * 8)
    far_out = ffn([far[0][0], far[0][1], far[1][0], far[1][1]], weights, (64,) * 4)

    back = []
    for k, (one, two, _) in enumerate(order):
        l0, l1, r0, r1 = near_out[4 * k : 4 * k + 4]
        o0, o1 = far_out[2 * k : 2 * k + 2]
        u1 = shift(r1, two, 1)
        u2 = shift(l0, two, -1)
        t1 = shift(o0, two, 1)
        t2 = shift(o1, two, -1)
        v1 = shift(add(r0, t1), two, 1)
        v2 = shift(add(l1, t2), two, -1)
        s = own_out[k].astype(F32)
        upper = s[:64] + v1.astype(F32) + u2.astype(F32)
        lower = s[64:] + u1.astype(F32) + v2.astype(F32)
        back.append((upper.astype(BF), lower.astype(BF)))
    ends = []
    for k, (one, two, _) in enumerate(order):
        upper, lower = back[k]
        ends.append(
            (
                upper[:32],
                shift(upper[32:], one, -1),
                shift(lower[:32], one, 1),
                shift(lower[32:], one, 2),
            )
        )
    final = last(place, slot_owner, draft_len, hc_res, hc_out, first, ends[0], ends[1])
    new_streams = (
        final.reshape(SLOTS, Q, LT, NS, 128).transpose(0, 1, 3, 2, 4).reshape(SLOTS, Q, NS, D)
    )
    accepted_kv = (
        kv.reshape(SLOTS, DRAFT, 4, 2, 128).transpose(0, 1, 3, 2, 4).reshape(SLOTS, DRAFT, 2, 512)
    )
    return (new_streams, accepted_kv)


def solution(mesh):
    placed = (
        P("req", None, None, None),
        P(None, "head"),
        P(None, "head"),
        P(None, "head"),
        P("head", None),
        P(None, "req"),
        P(None, "req"),
        P("req", None),
        P("req", None, "head"),
        P("req", None, "head"),
        P(),
        P(),
        P(),
        P(),
        P(),
        P(),
        P(),
        P(),
    )
    return jax.shard_map(
        body,
        mesh=mesh,
        in_specs=placed,
        out_specs=(P("req", "head", None, None), P("req", None, None, "head")),
        check_vma=False,
    )
```

```python
import functools

import jax
import jax.numpy as jnp
import numpy as np
from jax import lax
from jax.experimental import pallas as pl
from jax.experimental.pallas import tpu as pltpu
from jax.sharding import PartitionSpec as P

HD = 128
SLOTS = 4
DRAFT = 64
CACHE = 1024
D = 2048
NS = 4
LT = D // 128
Q = 16
SCALE = HD ** (-0.5)
BF = jnp.bfloat16
F32 = jnp.float32
BLOCKS = 8
PACKED = 3072
OFFSETS = ((1, 1), (-1, -1), (1, -1), (-1, 1), (2, 0), (0, 2), (2, 2))
MEMBERS = len(OFFSETS) + 1
FIRST = 4
NT = (((1,), (1,)), ((), ()))


def mm(a, b):
    return jnp.dot(a, b, preferred_element_type=F32)


def mm_nt(a, b):
    return lax.dot_general(a, b, NT, preferred_element_type=F32)


def normalize(x):
    center = jnp.sum(x, axis=-1, keepdims=True) * (1.0 / D)
    y = x - center
    spread = jnp.sum(y * y, axis=-1, keepdims=True) * (1.0 / D)
    return y * lax.rsqrt(spread + 1e-05)


def front_kernel(
    place,
    owner,
    dlen,
    clen,
    pick,
    hc_in,
    parents,
    freq,
    st,
    wq,
    wk,
    wv,
    ck,
    cv,
    wo,
    out,
    kv_out,
    raw,
    xbuf,
    normed,
    above_s,
    take_s,
    cos_s,
    sin_s,
    att,
    acc,
    kvs,
):
    i = pl.program_id(0)
    base = place[0] * SLOTS

    @pl.when(i < SLOTS)
    def _():
        s = i
        r = owner[base + s]
        raw[...] = st[...].astype(F32)
        rows = DRAFT
        for j in range(LT):
            x = hc_in[0, 0] * raw[pl.ds(j * NS, rows, stride=LT * NS), :]
            for m in range(1, NS):
                x = x + hc_in[0, m] * raw[pl.ds(j * NS + m, rows, stride=LT * NS), :]
            xbuf[:, j * 128 : (j + 1) * 128] = x
        normed[pl.ds(pl.multiple_of(s * DRAFT, DRAFT), DRAFT), :] = normalize(xbuf[...]).astype(BF)
        par = parents[pl.ds(r, 1), :]
        qi = lax.broadcasted_iota(jnp.int32, (DRAFT, DRAFT), 0)
        pi = lax.broadcasted_iota(jnp.int32, (DRAFT, DRAFT), 1)
        eye = (qi == pi).astype(F32)
        up = jnp.where(par == qi, 1.0, eye)
        for rounds in range(6):
            b = up.astype(BF)
            up = jnp.minimum(mm(b, b), 1.0)
        above = mm_nt(eye.astype(BF), up.astype(BF))
        above_s[s] = above
        depth_row = jnp.sum(up, axis=0, keepdims=True) - 1.0
        depth = jnp.sum(above, axis=1, keepdims=True) - 1.0
        a = jnp.minimum(pick[r], dlen[r] - 1)
        path = above_s[s, pl.ds(a, 1), :]
        take = jnp.where(depth_row == qi.astype(F32), path, 0.0)
        take_s[s] = take.astype(BF)
        angle = (clen[r].astype(F32) + depth) * freq[...]
        lane = lax.broadcasted_iota(jnp.int32, (DRAFT, HD), 1)
        at = pl.ds(pl.multiple_of(s * DRAFT, DRAFT), DRAFT)
        cos_s[at, :] = jnp.cos(angle)
        sine = jnp.sin(angle)
        sin_s[at, :] = jnp.where(lane < HD // 2, -sine, sine)

    @pl.when(i >= SLOTS)
    def _():
        g = i - SLOTS
        x = normed[...]
        q2 = mm(x, wq[...])
        k2 = mm(x, wk[...])
        v2 = mm(x, wv[...]).astype(BF)
        cosine = cos_s[...]
        sine = sin_s[...]
        col = lax.broadcasted_iota(jnp.int32, (DRAFT, CACHE), 1)
        for hh in range(2):
            cols = slice(hh * HD, (hh + 1) * HD)
            qh = q2[:, cols]
            kh = k2[:, cols]
            qh = (qh * cosine + pltpu.roll(qh, HD // 2, 1) * sine).astype(BF)
            kh = (kh * cosine + pltpu.roll(kh, HD // 2, 1) * sine).astype(BF)
            vh = v2[:, cols]
            for s in range(SLOTS):
                at = slice(s * DRAFT, (s + 1) * DRAFT)
                length = clen[owner[base + s]]
                qs, ks, vs = qh[at], kh[at], vh[at]
                sc = mm_nt(qs, ck[s, :, cols]) * SCALE
                sc = jnp.where(col < length, sc, -1e30)
                lo = mm_nt(qs, ks) * SCALE
                lo = jnp.where(above_s[s] > 0.5, lo, -1e30)
                top = jnp.maximum(
                    jnp.max(sc, axis=-1, keepdims=True), jnp.max(lo, axis=-1, keepdims=True)
                )
                e1 = jnp.exp(sc - top)
                e2 = jnp.exp(lo - top)
                total = jnp.sum(e1, axis=-1, keepdims=True) + jnp.sum(e2, axis=-1, keepdims=True)
                inv = 1.0 / total
                w1 = (e1 * inv).astype(BF)
                w2 = (e2 * inv).astype(BF)
                o = mm(w1, cv[s, :, cols]) + mm(w2, vs)
                att[at, cols] = o.astype(BF)
                tk = take_s[s]
                kvs[s, pl.ds((g * 2 + hh) * 2, DRAFT, stride=8), :] = mm(tk, ks)
                kvs[s, pl.ds((g * 2 + hh) * 2 + 1, DRAFT, stride=8), :] = mm(tk, vs)
        part = mm(att[...], wo[...])

        @pl.when(g == 0)
        def _():
            acc[...] = part

        @pl.when(g == 1)
        def _():
            full = (acc[...] + part).astype(BF)
            for s in range(SLOTS):
                for y in range(4):
                    out[y, s * Q : (s + 1) * Q, :] = full[
                        s * DRAFT + y * Q : s * DRAFT + (y + 1) * Q
                    ]
                kv_out[s * 512 : (s + 1) * 512, :] = kvs[s].astype(BF)


def front(place, owner, dlen, clen, pick, hc_in, parents, freq, st, wq, wk, wv, ck, cv, wo):
    smem = pl.BlockSpec(memory_space=pltpu.SMEM)
    head = lambda i, *_: (0, jnp.maximum(i - SLOTS, 0))
    cache = lambda i, *_: (0, 0, jnp.maximum(i - SLOTS, 0))
    return pl.pallas_call(
        front_kernel,
        name="front",
        out_shape=(
            jax.ShapeDtypeStruct((4, SLOTS * Q, D), BF),
            jax.ShapeDtypeStruct((2048, 128), BF),
        ),
        grid_spec=pltpu.PrefetchScalarGridSpec(
            num_scalar_prefetch=5,
            grid=(SLOTS + 2,),
            in_specs=[
                smem,
                pl.BlockSpec((128, DRAFT), lambda i, *_: (0, 0)),
                pl.BlockSpec((1, HD), lambda i, *_: (0, 0)),
                pl.BlockSpec((4096, 128), lambda i, *_: (jnp.minimum(i, SLOTS - 1), 0)),
                pl.BlockSpec((D, 256), head),
                pl.BlockSpec((D, 256), head),
                pl.BlockSpec((D, 256), head),
                pl.BlockSpec((SLOTS, CACHE, 256), cache),
                pl.BlockSpec((SLOTS, CACHE, 256), cache),
                pl.BlockSpec((256, D), lambda i, *_: (jnp.maximum(i - SLOTS, 0), 0)),
            ],
            out_specs=[
                pl.BlockSpec((4, SLOTS * Q, D), lambda i, *_: (0, 0, 0)),
                pl.BlockSpec((2048, 128), lambda i, *_: (0, 0)),
            ],
            scratch_shapes=[
                pltpu.VMEM((4096, 128), F32),
                pltpu.VMEM((DRAFT, D), F32),
                pltpu.VMEM((SLOTS * DRAFT, D), BF),
                pltpu.VMEM((SLOTS, DRAFT, DRAFT), F32),
                pltpu.VMEM((SLOTS, DRAFT, DRAFT), BF),
                pltpu.VMEM((SLOTS * DRAFT, HD), F32),
                pltpu.VMEM((SLOTS * DRAFT, HD), F32),
                pltpu.VMEM((SLOTS * DRAFT, 256), BF),
                pltpu.VMEM((SLOTS * DRAFT, D), F32),
                pltpu.VMEM((SLOTS, 512, 128), F32),
            ],
        ),
        compiler_params=pltpu.CompilerParams(vmem_limit_bytes=56 * 2**20),
    )(place, owner, dlen, clen, pick, hc_in, parents, freq, st, wq, wk, wv, ck, cv, wo)


def mid_kernel(place, hc_in, hc_res, hc_out, parts, st, first, rows, raw, xbuf):
    raw[...] = st[...].astype(F32)
    for j in range(LT):
        lanes = slice(j * 128, (j + 1) * 128)
        attn = parts[0, :, lanes].astype(F32)
        for y in range(1, 4):
            attn = attn + parts[y, :, lanes].astype(F32)
        own = [raw[pl.ds(j * NS + n, Q, stride=LT * NS), :] for n in range(NS)]
        x = None
        for m in range(NS):
            c = hc_out[0, m] * attn
            for n in range(NS):
                c = c + hc_res[0, n, m] * own[n]
            c = c.astype(BF)
            first[m, :, lanes] = c
            t = hc_in[1, m] * c.astype(F32)
            x = t if x is None else x + t
        xbuf[:, lanes] = x
    rows[...] = normalize(xbuf[...]).astype(BF)


def mid(place, hc_in, hc_res, hc_out, parts, st):
    smem = pl.BlockSpec(memory_space=pltpu.SMEM)
    return pl.pallas_call(
        mid_kernel,
        name="mid",
        out_shape=(
            jax.ShapeDtypeStruct((NS, SLOTS * Q, D), BF),
            jax.ShapeDtypeStruct((SLOTS * Q, D), BF),
        ),
        grid_spec=pltpu.PrefetchScalarGridSpec(
            num_scalar_prefetch=1,
            grid=(SLOTS,),
            in_specs=[
                smem,
                smem,
                smem,
                pl.BlockSpec((4, Q, D), lambda i, p: (0, i, 0)),
                pl.BlockSpec((1024, 128), lambda i, p: (i * 4 + p[1], 0)),
            ],
            out_specs=[
                pl.BlockSpec((NS, Q, D), lambda i, p: (0, i, 0)),
                pl.BlockSpec((Q, D), lambda i, p: (i, 0)),
            ],
            scratch_shapes=[pltpu.VMEM((1024, 128), F32), pltpu.VMEM((Q, D), F32)],
        ),
    )(place, hc_in, hc_res, hc_out, parts, st)


def last_kernel(place, owner, dlen, hc_res, hc_out, first, *refs):
    parts, out, raw = refs[:MEMBERS], refs[MEMBERS], refs[MEMBERS + 1]
    i = pl.program_id(0)
    count = dlen[owner[place[0] * SLOTS + i]]
    spot = place[1] * Q + lax.broadcasted_iota(jnp.int32, (Q, 128), 0)
    alive = spot < count
    for j in range(LT):
        lanes = slice(j * 128, (j + 1) * 128)
        mlp = parts[0][:, lanes].astype(F32)
        for p in parts[1:]:
            mlp = mlp + p[:, lanes].astype(F32)
        f = [first[n, :, lanes].astype(F32) for n in range(NS)]
        for m in range(NS):
            c = hc_out[1, m] * mlp
            for n in range(NS):
                c = c + hc_res[1, n, m] * f[n]
            raw[pl.ds(j * NS + m, Q, stride=LT * NS), :] = jnp.where(alive, c, 0.0)
    out[...] = raw[...].astype(BF)


def last(place, owner, dlen, hc_res, hc_out, first, parts):
    smem = pl.BlockSpec(memory_space=pltpu.SMEM)
    return pl.pallas_call(
        last_kernel,
        name="last",
        out_shape=jax.ShapeDtypeStruct((SLOTS * 1024, 128), BF),
        grid_spec=pltpu.PrefetchScalarGridSpec(
            num_scalar_prefetch=3,
            grid=(SLOTS,),
            in_specs=[smem, smem, pl.BlockSpec((NS, Q, D), lambda i, *_: (0, i, 0))]
            + [pl.BlockSpec((Q, D), lambda i, *_: (i, 0))] * MEMBERS,
            out_specs=pl.BlockSpec((1024, 128), lambda i, *_: (i, 0)),
            scratch_shapes=[pltpu.VMEM((1024, 128), F32)],
        ),
    )(place, owner, dlen, hc_res, hc_out, first, *parts)


def pack_kernel(g, u, d, one, two):
    for k, w in enumerate((one, two)):
        lanes = slice(k * 128, (k + 1) * 128)
        w[0:512, 0:128] = g[:, lanes]
        w[0:512, 128:256] = u[:, lanes]
        w[512:640, :] = d[lanes, 0:256]
        w[640:768, :] = d[lanes, 256:512]


def pack(g, u, d):
    tall = pl.BlockSpec((512, 256), lambda j: (j, 0))
    packed = pl.BlockSpec((768, 256), lambda j: (j, 0))
    return pl.pallas_call(
        pack_kernel,
        name="pack",
        grid=(4,),
        out_shape=(jax.ShapeDtypeStruct((PACKED, 256), BF),) * 2,
        in_specs=[tall, tall, pl.BlockSpec((256, 512), lambda j: (0, j))],
        out_specs=(packed, packed),
    )(g, u, d)


def ffn_kernel(n, *refs):
    xs, ws, ys = refs[:n], refs[n : n + BLOCKS], refs[n + BLOCKS : 2 * n + BLOCKS]
    cat, wbuf, inner, sems = refs[2 * n + BLOCKS :]
    rows = SLOTS * Q
    arrive = [
        pltpu.make_async_copy(x, cat.at[pl.ds(k * rows, rows), :], sems.at[BLOCKS + k])
        for k, x in enumerate(xs)
    ]
    copies = [pltpu.make_async_copy(w, wbuf.at[k], sems.at[k]) for k, w in enumerate(ws)]
    for c in arrive + copies:
        c.start()
    for c in arrive:
        c.wait()
    for k in range(BLOCKS):
        copies[k].wait()
        both = None
        for j in range(4):
            t = mm(cat[:, 512 * j : 512 * (j + 1)], wbuf[k, 768 * j : 768 * j + 512, :])
            both = t if both is None else both + t
        gate = both[:, :128]
        inner[:, k * 128 : (k + 1) * 128] = (gate / (1.0 + jnp.exp(-gate)) * both[:, 128:]).astype(
            BF
        )
    h = inner[...]
    for c in range(8):
        at = 768 * (c // 2) + 512 + 128 * (c % 2)
        down = jnp.concatenate([wbuf[k, at : at + 128, :] for k in range(BLOCKS)], axis=0)
        t = mm(h, down).astype(BF)
        for k in range(n):
            ys[k][:, 256 * c : 256 * (c + 1)] = t[k * rows : (k + 1) * rows]


def ffn(xs, weights):
    n = len(xs)
    vmem = pl.BlockSpec(memory_space=pltpu.VMEM)
    rows = n * SLOTS * Q
    return pl.pallas_call(
        functools.partial(ffn_kernel, n),
        name="ffn",
        out_shape=tuple(jax.ShapeDtypeStruct((SLOTS * Q, D), BF) for _ in xs),
        in_specs=[pl.BlockSpec(memory_space=pl.ANY)] * (n + BLOCKS),
        out_specs=tuple([vmem] * n),
        scratch_shapes=[
            pltpu.VMEM((rows, D), BF),
            pltpu.VMEM((BLOCKS, PACKED, 256), BF),
            pltpu.VMEM((rows, 128 * BLOCKS), BF),
            pltpu.SemaphoreType.DMA((BLOCKS + n,)),
        ],
        cost_estimate=pl.CostEstimate(
            flops=rows * D * 1024 * 6, transcendentals=rows * 1024, bytes_accessed=rows * D * 4
        ),
        compiler_params=pltpu.CompilerParams(vmem_limit_bytes=56 * 2**20),
    )(*xs, *weights)


def pairs(move):
    out = []
    for x in range(4):
        for z in range(4):
            for c in range(2):
                tx, tz, tc = move(x, z, c)
                out.append((x * 8 + z * 2 + c, (tx % 4) * 8 + (tz % 4) * 2 + tc))
    return out


def send(v, move):
    return lax.ppermute(v, "req", pairs(move))


def shift(v, dx, dz):
    return send(v, lambda x, z, c: (x + dx, z + dz, c))


def other_core(v):
    return send(v, lambda x, z, c: (x, z, 1 - c))


def body(
    streams,
    w_query,
    w_key,
    w_value,
    w_output,
    w_gate,
    w_up,
    w_down,
    cache_keys,
    cache_values,
    hc_in,
    hc_res,
    hc_out,
    parents,
    draft_len,
    cache_len,
    accept_pick,
    slot_owner,
):
    place = jnp.stack([lax.axis_index("req"), lax.axis_index("head")]).astype(jnp.int32)
    half = np.arange(64, dtype=np.float64)
    freq = np.power(10000.0, -(half * 2.0 / HD)).astype(np.float32)
    freq = jnp.asarray(np.concatenate([freq, freq])[None, :])
    st = streams.reshape(SLOTS, DRAFT, NS, LT, 128).transpose(0, 1, 3, 2, 4).reshape(-1, 128)
    one, two = pack(w_gate, w_up, w_down)
    one_z = send(one, lambda x, z, c: (x, z ^ 1, c))
    two_x = send(two, lambda x, z, c: (x ^ 1, z, c))
    weights = (one, two, other_core(one), other_core(two))
    part, kv = front(
        place,
        slot_owner,
        draft_len,
        cache_len,
        accept_pick,
        hc_in,
        parents,
        freq,
        st,
        w_query,
        w_key,
        w_value,
        cache_keys,
        cache_values,
        w_output,
    )
    part, one_z, two_x = lax.optimization_barrier((part, one_z, two_x))
    parts = lax.all_to_all(part, "head", 0, 0, tiled=False)
    weights = weights + (one_z, two_x, other_core(one_z), other_core(two_x))
    parts, weights = lax.optimization_barrier((parts, weights))
    first, rows = mid(place, hc_in, hc_res, hc_out, parts, st)
    pieces = [rows] + [shift(rows, dx, dz) for dx, dz in OFFSETS]
    sums = ffn(pieces[:FIRST], weights) + ffn(pieces[FIRST:], weights)
    back = [sums[0]] + [shift(t, -dx, -dz) for t, (dx, dz) in zip(sums[1:], OFFSETS)]
    final = last(place, slot_owner, draft_len, hc_res, hc_out, first, back)
    new_streams = (
        final.reshape(SLOTS, Q, LT, NS, 128).transpose(0, 1, 3, 2, 4).reshape(SLOTS, Q, NS, D)
    )
    accepted_kv = (
        kv.reshape(SLOTS, DRAFT, 4, 2, 128).transpose(0, 1, 3, 2, 4).reshape(SLOTS, DRAFT, 2, 512)
    )
    return (new_streams, accepted_kv)


def solution(mesh):
    placed = (
        P("req", None, None, None),
        P(None, "head"),
        P(None, "head"),
        P(None, "head"),
        P("head", None),
        P(None, "req"),
        P(None, "req"),
        P("req", None),
        P("req", None, "head"),
        P("req", None, "head"),
        P(),
        P(),
        P(),
        P(),
        P(),
        P(),
        P(),
        P(),
    )
    return jax.shard_map(
        body,
        mesh=mesh,
        in_specs=placed,
        out_specs=(P("req", "head", None, None), P("req", None, None, "head")),
        check_vma=False,
    )
```

```python
import functools

import jax
import jax.numpy as jnp
import numpy as np
from jax import lax
from jax.experimental import pallas as pl
from jax.experimental.pallas import tpu as pltpu
from jax.sharding import PartitionSpec as P

HD = 128
SLOTS = 4
DRAFT = 64
CACHE = 1024
D = 2048
NS = 4
LT = D // 128
Q = 16
SCALE = HD ** (-0.5)
BF = jnp.bfloat16
F32 = jnp.float32
BLOCKS = 8
PITCH = 72
PACKED = 3072
OFFSETS = ((1, 1), (-1, -1), (1, -1), (-1, 1), (2, 0), (0, 2), (2, 2))
MEMBERS = len(OFFSETS) + 1
FIRST = 4
CH = 4
NT = (((1,), (1,)), ((), ()))


def near(x):
    return pltpu.with_memory_space_constraint(x, pltpu.VMEM)


def mm(a, b):
    return jnp.dot(a, b, preferred_element_type=F32)


def mm_nt(a, b):
    return lax.dot_general(a, b, NT, preferred_element_type=F32)


def normalize(x):
    center = jnp.sum(x, axis=-1, keepdims=True) * (1.0 / D)
    y = x - center
    spread = jnp.sum(y * y, axis=-1, keepdims=True) * (1.0 / D)
    return y * lax.rsqrt(spread + 1e-05)


def front_kernel(
    place,
    owner,
    dlen,
    clen,
    pick,
    hc_in,
    parents,
    freq,
    st,
    wq_h,
    wk_h,
    wv_h,
    wo_h,
    ck_h,
    cv_h,
    out0,
    out1,
    out2,
    out3,
    own,
    kv_out,
    raw,
    xbuf,
    normed,
    above_s,
    take_s,
    cos_s,
    sin_s,
    att,
    acc,
    kvs,
    wq,
    wk,
    wv,
    wo,
    ck,
    cv,
    sems,
):
    i = pl.program_id(0)
    base = place[0] * SLOTS

    def loads(g):
        cols = pl.ds(g * 256, 256)
        return (
            pltpu.make_async_copy(wq_h.at[:, cols], wq.at[g], sems.at[g, 0]),
            pltpu.make_async_copy(wk_h.at[:, cols], wk.at[g], sems.at[g, 1]),
            pltpu.make_async_copy(wv_h.at[:, cols], wv.at[g], sems.at[g, 2]),
            pltpu.make_async_copy(ck_h.at[:, :, cols], ck.at[g], sems.at[g, 3]),
            pltpu.make_async_copy(cv_h.at[:, :, cols], cv.at[g], sems.at[g, 4]),
            pltpu.make_async_copy(wo_h.at[cols, :], wo.at[g], sems.at[g, 5]),
        )

    @pl.when(i == 0)
    def _():
        for c in loads(0):
            c.start()

    @pl.when(i == 1)
    def _():
        for c in loads(1):
            c.start()

    @pl.when(i == 0)
    def _():
        pi = lax.broadcasted_iota(jnp.int32, (DRAFT, DRAFT), 0)
        qi = lax.broadcasted_iota(jnp.int32, (DRAFT, DRAFT), 1)
        eye = (qi == pi).astype(F32)
        who = lax.broadcasted_iota(jnp.int32, (DRAFT, 128), 1)
        lane = lax.broadcasted_iota(jnp.int32, (DRAFT, HD), 1)
        ones = jnp.ones((8, DRAFT), BF)
        ups = []
        for s in range(SLOTS):
            r = owner[base + s]
            par = jnp.sum(jnp.where(who == r, parents[...], 0), axis=1, keepdims=True)
            ups.append(jnp.where(par == qi, 1.0, eye))
        for rounds in range(6):
            nxt = []
            for up in ups:
                b = up.astype(BF)
                nxt.append(jnp.minimum(mm(b, b), 1.0))
            ups = nxt
        for s in range(SLOTS):
            r = owner[base + s]
            above = ups[s]
            above_s[s] = above
            depth_row = mm_nt(ones, above.astype(BF))[0:1] - 1.0
            depth = jnp.sum(above, axis=1, keepdims=True) - 1.0
            a = jnp.minimum(pick[r], dlen[r] - 1)
            path = above_s[s, pl.ds(a, 1), :]
            take = jnp.where(depth_row == pi.astype(F32), path, 0.0)
            take_s[s] = take.astype(BF)
            angle = (clen[r].astype(F32) + depth) * freq[...]
            at = slice(s * DRAFT, (s + 1) * DRAFT)
            cos_s[at, :] = jnp.cos(angle)
            sine = jnp.sin(angle)
            sin_s[at, :] = jnp.where(lane < HD // 2, -sine, sine)

    @pl.when(i < SLOTS)
    def _():
        s = i
        for p in range(DRAFT):
            raw[p * PITCH : p * PITCH + 64, :] = st[p * 64 : (p + 1) * 64, :].astype(F32)
        total = None
        for j in range(LT):
            x = hc_in[0, 0] * raw[pl.ds(j * NS, DRAFT, stride=PITCH), :]
            for m in range(1, NS):
                x = x + hc_in[0, m] * raw[pl.ds(j * NS + m, DRAFT, stride=PITCH), :]
            xbuf[:, j * 128 : (j + 1) * 128] = x
            total = x if total is None else total + x
        for j in range(LT):
            for n in range(NS):
                own[n, pl.ds(pl.multiple_of(s * Q, Q), Q), j * 128 : (j + 1) * 128] = raw[
                    pl.ds(place[1] * (Q * PITCH) + j * NS + n, Q, stride=PITCH), :
                ].astype(BF)
        center = jnp.sum(total, axis=-1, keepdims=True) * (1.0 / D)
        y = xbuf[...] - center
        spread = jnp.sum(y * y, axis=-1, keepdims=True) * (1.0 / D)
        normed[pl.ds(pl.multiple_of(s * DRAFT, DRAFT), DRAFT), :] = (
            y * lax.rsqrt(spread + 1e-05)
        ).astype(BF)

    def heads(g):
        arrive = loads(g)
        for c in arrive[:3]:
            c.wait()
        x = normed[...]
        q2 = mm(x, wq[g])
        k2 = mm(x, wk[g])
        v2 = mm(x, wv[g]).astype(BF)
        cosine = cos_s[...]
        sine = sin_s[...]
        col = lax.broadcasted_iota(jnp.int32, (DRAFT, CACHE), 1)
        for c in arrive[3:]:
            c.wait()
        for hh in range(2):
            cols = slice(hh * HD, (hh + 1) * HD)
            qh = q2[:, cols]
            kh = k2[:, cols]
            qh = (qh * cosine + pltpu.roll(qh, HD // 2, 1) * sine).astype(BF)
            kh = (kh * cosine + pltpu.roll(kh, HD // 2, 1) * sine).astype(BF)
            vh = v2[:, cols]
            for s in range(SLOTS):
                at = slice(s * DRAFT, (s + 1) * DRAFT)
                length = clen[owner[base + s]]
                qs, ks, vs = qh[at], kh[at], vh[at]
                sc = mm_nt(qs, ck[g, s, :, cols]) * SCALE
                sc = jnp.where(col < length, sc, -1e30)
                lo = mm_nt(qs, ks) * SCALE
                lo = jnp.where(above_s[s] > 0.5, lo, -1e30)
                top = jnp.maximum(
                    jnp.max(sc, axis=-1, keepdims=True), jnp.max(lo, axis=-1, keepdims=True)
                )
                e1 = jnp.exp(sc - top)
                e2 = jnp.exp(lo - top)
                total = jnp.sum(e1, axis=-1, keepdims=True) + jnp.sum(e2, axis=-1, keepdims=True)
                inv = 1.0 / total
                w1 = (e1 * inv).astype(BF)
                w2 = (e2 * inv).astype(BF)
                o = mm(w1, cv[g, s, :, cols]) + mm(w2, vs)
                att[at, cols] = o.astype(BF)
                tk = take_s[s]
                h = g * 2 + hh
                kvs[s, pl.ds(h * 2, DRAFT, stride=8), :] = mm(tk, ks)
                kvs[s, pl.ds(h * 2 + 1, DRAFT, stride=8), :] = mm(tk, vs)
        part = mm(att[...], wo[g])
        if g == 0:
            acc[...] = part
        else:
            acc[...] = acc[...] + part
            for s in range(SLOTS):
                for k, out in enumerate((out0, out1, out2, out3)):
                    from_row = s * DRAFT + lax.rem(place[1] + k, 4) * Q
                    out[s * Q : (s + 1) * Q, :] = acc[
                        pl.ds(pl.multiple_of(from_row, Q), Q), :
                    ].astype(BF)
                kv_out[s * 512 : (s + 1) * 512, :] = kvs[s].astype(BF)

    @pl.when(i == SLOTS - 1)
    def _():
        heads(0)
        heads(1)


def front(place, owner, dlen, clen, pick, hc_in, parents, freq, st, wq, wk, wv, ck, cv, wo):
    smem = pl.BlockSpec(memory_space=pltpu.SMEM)
    vmem = pl.BlockSpec(memory_space=pltpu.VMEM)
    return pl.pallas_call(
        front_kernel,
        name="front",
        out_shape=(pltpu.VMEM((SLOTS * Q, D), BF),) * 4
        + (
            pltpu.VMEM((NS, SLOTS * Q, D), BF),
            jax.ShapeDtypeStruct((2048, 128), BF),
        ),
        grid_spec=pltpu.PrefetchScalarGridSpec(
            num_scalar_prefetch=5,
            grid=(SLOTS,),
            in_specs=[
                smem,
                pl.BlockSpec((DRAFT, 128), lambda i, *_: (0, 0)),
                pl.BlockSpec((1, HD), lambda i, *_: (0, 0)),
                pl.BlockSpec((4096, 128), lambda i, *_: (i, 0)),
            ]
            + [pl.BlockSpec(memory_space=pltpu.HBM)] * 6,
            out_specs=[vmem] * 5 + [pl.BlockSpec((2048, 128), lambda i, *_: (0, 0))],
            scratch_shapes=[
                pltpu.VMEM((DRAFT * PITCH, 128), F32),
                pltpu.VMEM((DRAFT, D), F32),
                pltpu.VMEM((SLOTS * DRAFT, D), BF),
                pltpu.VMEM((SLOTS, DRAFT, DRAFT), F32),
                pltpu.VMEM((SLOTS, DRAFT, DRAFT), BF),
                pltpu.VMEM((SLOTS * DRAFT, HD), F32),
                pltpu.VMEM((SLOTS * DRAFT, HD), F32),
                pltpu.VMEM((SLOTS * DRAFT, 256), BF),
                pltpu.VMEM((SLOTS * DRAFT, D), F32),
                pltpu.VMEM((SLOTS, 512, 128), F32),
                pltpu.VMEM((2, D, 256), BF),
                pltpu.VMEM((2, D, 256), BF),
                pltpu.VMEM((2, D, 256), BF),
                pltpu.VMEM((2, 256, D), BF),
                pltpu.VMEM((2, SLOTS, CACHE, 256), BF),
                pltpu.VMEM((2, SLOTS, CACHE, 256), BF),
                pltpu.SemaphoreType.DMA((2, 6)),
            ],
        ),
        compiler_params=pltpu.CompilerParams(vmem_limit_bytes=36 * 2**20),
    )(
        place,
        owner,
        dlen,
        clen,
        pick,
        hc_in,
        parents,
        freq,
        pltpu.with_memory_space_constraint(st, pltpu.HBM),
        *[pltpu.with_memory_space_constraint(x, pltpu.HBM) for x in (wq, wk, wv, wo, ck, cv)],
    )


def mid_kernel(hc_in, hc_res, hc_out, p0, p1, p2, p3, own, first, rows, xbuf):
    for s in range(SLOTS):
        at = slice(s * Q, (s + 1) * Q)
        total = None
        for j in range(LT):
            lanes = slice(j * 128, (j + 1) * 128)
            attn = p0[at, lanes].astype(F32)
            for p in (p1, p2, p3):
                attn = attn + p[at, lanes].astype(F32)
            mine = [own[n, at, lanes].astype(F32) for n in range(NS)]
            x = None
            for m in range(NS):
                c = hc_out[0, m] * attn
                for n in range(NS):
                    c = c + hc_res[0, n, m] * mine[n]
                c = c.astype(BF)
                first[m, at, lanes] = c
                t = hc_in[1, m] * c.astype(F32)
                x = t if x is None else x + t
            xbuf[at, lanes] = x
            total = x if total is None else total + x
        center = jnp.sum(total, axis=-1, keepdims=True) * (1.0 / D)
        y = xbuf[at, :] - center
        spread = jnp.sum(y * y, axis=-1, keepdims=True) * (1.0 / D)
        rows[at, :] = (y * lax.rsqrt(spread + 1e-05)).astype(BF)


def mid(hc_in, hc_res, hc_out, parts, own):
    smem = pl.BlockSpec(memory_space=pltpu.SMEM)
    vmem = pl.BlockSpec(memory_space=pltpu.VMEM)
    return pl.pallas_call(
        mid_kernel,
        name="mid",
        out_shape=(pltpu.VMEM((NS, SLOTS * Q, D), BF), pltpu.VMEM((SLOTS * Q, D), BF)),
        in_specs=[smem] * 3 + [vmem] * 5,
        out_specs=(vmem, vmem),
        scratch_shapes=[pltpu.VMEM((SLOTS * Q, D), F32)],
        compiler_params=pltpu.CompilerParams(vmem_limit_bytes=8 * 2**20),
    )(hc_in, hc_res, hc_out, *[near(p) for p in parts], near(own))


def last_kernel(place, owner, dlen, hc_res, hc_out, first, *refs):
    parts, out, raw = refs[:MEMBERS], refs[MEMBERS], refs[MEMBERS + 1]
    spot = place[1] * Q + lax.broadcasted_iota(jnp.int32, (Q, 128), 0)
    for s in range(SLOTS):
        at = slice(s * Q, (s + 1) * Q)
        alive = spot < dlen[owner[place[0] * SLOTS + s]]
        for j in range(LT):
            lanes = slice(j * 128, (j + 1) * 128)
            mlp = parts[0][at, lanes].astype(F32)
            for p in parts[1:]:
                mlp = mlp + p[at, lanes].astype(F32)
            f = [first[n, at, lanes].astype(F32) for n in range(NS)]
            for m in range(NS):
                c = hc_out[1, m] * mlp
                for n in range(NS):
                    c = c + hc_res[1, n, m] * f[n]
                raw[pl.ds(j * NS + m, Q, stride=PITCH), :] = jnp.where(alive, c, 0.0)
        for p in range(Q):
            out[(s * Q + p) * 64 : (s * Q + p + 1) * 64, :] = raw[
                p * PITCH : p * PITCH + 64, :
            ].astype(BF)


def last(place, owner, dlen, hc_res, hc_out, first, parts):
    smem = pl.BlockSpec(memory_space=pltpu.SMEM)
    vmem = pl.BlockSpec(memory_space=pltpu.VMEM)
    return pl.pallas_call(
        last_kernel,
        name="last",
        out_shape=jax.ShapeDtypeStruct((SLOTS * 1024, 128), BF),
        in_specs=[smem] * 5 + [vmem] * (1 + MEMBERS),
        out_specs=vmem,
        scratch_shapes=[pltpu.VMEM((Q * PITCH, 128), F32)],
        compiler_params=pltpu.CompilerParams(vmem_limit_bytes=8 * 2**20),
    )(place, owner, dlen, hc_res, hc_out, near(first), *[near(p) for p in parts])


def pack_kernel(g, u, d, one, two, buf, sems):
    ins, outs = [], []
    for k, w in enumerate((one, two)):
        part = pl.ds(k * 128, 128)
        here = buf.at[k]
        ins.append(
            [
                pltpu.make_async_copy(
                    g.at[:, part], here.at[pl.ds(0, D), pl.ds(0, 128)], sems.at[k, 0]
                ),
                pltpu.make_async_copy(
                    u.at[:, part], here.at[pl.ds(0, D), pl.ds(128, 128)], sems.at[k, 1]
                ),
            ]
            + [
                pltpu.make_async_copy(
                    d.at[part, pl.ds(256 * c, 256)],
                    here.at[pl.ds(D + 128 * c, 128), :],
                    sems.at[k, 2 + c],
                )
                for c in range(8)
            ]
        )
        outs.append(pltpu.make_async_copy(here, w, sems.at[k, 10]))
    for k in range(2):
        for c in ins[k]:
            c.start()
    for k in range(2):
        for c in ins[k]:
            c.wait()
        outs[k].start()
    for k in range(2):
        outs[k].wait()


def pack(g, u, d):
    hbm = pl.BlockSpec(memory_space=pltpu.HBM)
    return pl.pallas_call(
        pack_kernel,
        name="pack",
        out_shape=(jax.ShapeDtypeStruct((PACKED, 256), BF),) * 2,
        in_specs=[hbm] * 3,
        out_specs=(hbm, hbm),
        scratch_shapes=[pltpu.VMEM((2, PACKED, 256), BF), pltpu.SemaphoreType.DMA((2, 11))],
    )(*[pltpu.with_memory_space_constraint(x, pltpu.HBM) for x in (g, u, d)])


def ffn_kernel(n, *refs):
    xs, ws, ys = refs[:n], refs[n : n + BLOCKS], refs[n + BLOCKS : 2 * n + BLOCKS]
    cat, inner = refs[2 * n + BLOCKS :]
    rows = SLOTS * Q
    for k, x in enumerate(xs):
        cat[k * rows : (k + 1) * rows, :] = x[...]
    step = CH * rows
    spans = [(o, min(o + step, n * rows)) for o in range(0, n * rows, step)]
    for lo, hi in spans:
        for k, w in enumerate(ws):
            both = mm(cat[lo:hi, :], w[:D, :])
            gate = both[:, :128]
            inner[lo:hi, k * 128 : (k + 1) * 128] = (
                gate / (1.0 + jnp.exp(-gate)) * both[:, 128:]
            ).astype(BF)
        for c in range(8):
            at = D + 128 * c
            down = jnp.concatenate([w[at : at + 128, :] for w in ws], axis=0)
            t = mm(inner[lo:hi, :], down).astype(BF)
            for k in range(lo // rows, hi // rows):
                ys[k][:, 256 * c : 256 * (c + 1)] = t[k * rows - lo : (k + 1) * rows - lo]


def ffn(xs, weights):
    n = len(xs)
    vmem = pl.BlockSpec(memory_space=pltpu.VMEM)
    rows = n * SLOTS * Q
    return pl.pallas_call(
        functools.partial(ffn_kernel, n),
        name="ffn",
        out_shape=tuple(pltpu.VMEM((SLOTS * Q, D), BF) for _ in xs),
        in_specs=[vmem] * (n + BLOCKS),
        out_specs=tuple([vmem] * n),
        scratch_shapes=[
            pltpu.VMEM((rows, D), BF),
            pltpu.VMEM((rows, 128 * BLOCKS), BF),
        ],
        cost_estimate=pl.CostEstimate(
            flops=rows * D * 1024 * 6, transcendentals=rows * 1024, bytes_accessed=rows * D * 4
        ),
        compiler_params=pltpu.CompilerParams(vmem_limit_bytes=24 * 2**20),
    )(*[near(x) for x in xs], *[near(w) for w in weights])


def pairs(move):
    out = []
    for x in range(4):
        for z in range(4):
            for c in range(2):
                tx, tz, tc = move(x, z, c)
                out.append((x * 8 + z * 2 + c, (tx % 4) * 8 + (tz % 4) * 2 + tc))
    return out


def send(v, move):
    return lax.ppermute(v, "req", pairs(move))


def shift(v, dx, dz):
    return send(v, lambda x, z, c: (x + dx, z + dz, c))


def other_core(v):
    return send(v, lambda x, z, c: (x, z, 1 - c))


def body(
    streams,
    w_query,
    w_key,
    w_value,
    w_output,
    w_gate,
    w_up,
    w_down,
    cache_keys,
    cache_values,
    hc_in,
    hc_res,
    hc_out,
    parents,
    draft_len,
    cache_len,
    accept_pick,
    slot_owner,
):
    place = jnp.stack([lax.axis_index("req"), lax.axis_index("head")]).astype(jnp.int32)
    half = np.arange(64, dtype=np.float64)
    freq = np.power(10000.0, -(half * 2.0 / HD)).astype(np.float32)
    freq = jnp.asarray(np.concatenate([freq, freq])[None, :])
    st = streams.reshape(SLOTS, DRAFT, NS, LT, 128).transpose(0, 1, 3, 2, 4).reshape(-1, 128)
    one, two = pack(w_gate, w_up, w_down)
    one_z = send(one, lambda x, z, c: (x, z ^ 1, c))
    two_x = send(two, lambda x, z, c: (x ^ 1, z, c))
    weights = (one, two, other_core(one), other_core(two))
    *out, own, kv = front(
        place,
        slot_owner,
        draft_len,
        cache_len,
        accept_pick,
        hc_in,
        parents.T,
        freq,
        st,
        w_query,
        w_key,
        w_value,
        cache_keys,
        cache_values,
        w_output,
    )
    parts = [out[0]] + [
        lax.ppermute(out[k], "head", [(y, (y + k) % 4) for y in range(4)]) for k in (1, 3, 2)
    ]
    parts, one_z, two_x = lax.optimization_barrier((parts, one_z, two_x))
    weights = weights + (one_z, two_x, other_core(one_z), other_core(two_x))
    first, rows = mid(hc_in, hc_res, hc_out, [parts[0], parts[1], parts[3], parts[2]], own)
    rows, weights = lax.optimization_barrier((rows, weights))
    pieces = [rows] + [shift(rows, dx, dz) for dx, dz in OFFSETS]
    sums = ffn(pieces[:FIRST], weights) + ffn(pieces[FIRST:], weights)
    back = [sums[0]] + [shift(t, -dx, -dz) for t, (dx, dz) in zip(sums[1:], OFFSETS)]
    final = last(place, slot_owner, draft_len, hc_res, hc_out, first, back)
    new_streams = (
        final.reshape(SLOTS, Q, LT, NS, 128).transpose(0, 1, 3, 2, 4).reshape(SLOTS, Q, NS, D)
    )
    accepted_kv = (
        kv.reshape(SLOTS, DRAFT, 4, 2, 128).transpose(0, 1, 3, 2, 4).reshape(SLOTS, DRAFT, 2, 512)
    )
    return (new_streams, accepted_kv)


def solution(mesh):
    placed = (
        P("req", None, None, None),
        P(None, "head"),
        P(None, "head"),
        P(None, "head"),
        P("head", None),
        P(None, "req"),
        P(None, "req"),
        P("req", None),
        P("req", None, "head"),
        P("req", None, "head"),
        P(),
        P(),
        P(),
        P(),
        P(),
        P(),
        P(),
        P(),
    )
    return jax.shard_map(
        body,
        mesh=mesh,
        in_specs=placed,
        out_specs=(P("req", "head", None, None), P("req", None, None, "head")),
        check_vma=False,
    )
```

```python
import functools

import jax
import jax.numpy as jnp
import numpy as np
from jax import lax
from jax.experimental import pallas as pl
from jax.experimental.pallas import tpu as pltpu
from jax.sharding import PartitionSpec as P

HD = 128
SLOTS = 4
DRAFT = 64
CACHE = 1024
D = 2048
NS = 4
LT = D // 128
Q = 16
SCALE = HD ** (-0.5)
BF = jnp.bfloat16
F32 = jnp.float32
BLOCKS = 8
PITCH = 72
PACKED = 3072
OFFSETS = ((1, 1), (-1, -1), (1, -1), (-1, 1), (2, 0), (0, 2), (2, 2))
MEMBERS = len(OFFSETS) + 1
FIRST = 4
CH = 4
NT = (((1,), (1,)), ((), ()))


def near(x):
    return pltpu.with_memory_space_constraint(x, pltpu.VMEM)


def mm(a, b):
    return jnp.dot(a, b, preferred_element_type=F32)


def mm_nt(a, b):
    return lax.dot_general(a, b, NT, preferred_element_type=F32)


def normalize(x):
    center = jnp.sum(x, axis=-1, keepdims=True) * (1.0 / D)
    y = x - center
    spread = jnp.sum(y * y, axis=-1, keepdims=True) * (1.0 / D)
    return y * lax.rsqrt(spread + 1e-05)


def front_kernel(
    place,
    owner,
    dlen,
    clen,
    pick,
    hc_in,
    parents,
    freq,
    st,
    wq_h,
    wk_h,
    wv_h,
    wo_h,
    ck_h,
    cv_h,
    out0,
    out1,
    out2,
    out3,
    own,
    kv_out,
    raw,
    xbuf,
    normed,
    above_s,
    take_s,
    cos_s,
    sin_s,
    att,
    acc,
    kvs,
    wq,
    wk,
    wv,
    wo,
    ck,
    cv,
    sc_s,
    lo_s,
    w1_s,
    w2_s,
    sems,
):
    i = pl.program_id(0)
    base = place[0] * SLOTS

    def loads(g):
        cols = pl.ds(g * 256, 256)
        return (
            pltpu.make_async_copy(wq_h.at[:, cols], wq.at[g], sems.at[g, 0]),
            pltpu.make_async_copy(wk_h.at[:, cols], wk.at[g], sems.at[g, 1]),
            pltpu.make_async_copy(wv_h.at[:, cols], wv.at[g], sems.at[g, 2]),
            pltpu.make_async_copy(ck_h.at[:, :, cols], ck.at[g], sems.at[g, 3]),
            pltpu.make_async_copy(cv_h.at[:, :, cols], cv.at[g], sems.at[g, 4]),
            pltpu.make_async_copy(wo_h.at[cols, :], wo.at[g], sems.at[g, 5]),
        )

    @pl.when(i == 0)
    def _():
        for c in loads(0):
            c.start()

    @pl.when(i == SLOTS - 1)
    def _():
        for c in loads(1):
            c.start()

    @pl.when(i == 0)
    def _():
        pi = lax.broadcasted_iota(jnp.int32, (DRAFT, DRAFT), 0)
        qi = lax.broadcasted_iota(jnp.int32, (DRAFT, DRAFT), 1)
        eye = (qi == pi).astype(F32)
        who = lax.broadcasted_iota(jnp.int32, (DRAFT, 128), 1)
        lane = lax.broadcasted_iota(jnp.int32, (DRAFT, HD), 1)
        ones = jnp.ones((8, DRAFT), BF)
        ups = []
        for s in range(SLOTS):
            r = owner[base + s]
            par = jnp.sum(jnp.where(who == r, parents[...], 0), axis=1, keepdims=True)
            ups.append(jnp.where(par == qi, 1.0, eye))
        for rounds in range(6):
            nxt = []
            for up in ups:
                b = up.astype(BF)
                nxt.append(jnp.minimum(mm(b, b), 1.0))
            ups = nxt
        for s in range(SLOTS):
            r = owner[base + s]
            above = ups[s]
            above_s[s] = above
            depth_row = mm_nt(ones, above.astype(BF))[0:1] - 1.0
            depth = jnp.sum(above, axis=1, keepdims=True) - 1.0
            a = jnp.minimum(pick[r], dlen[r] - 1)
            path = above_s[s, pl.ds(a, 1), :]
            take = jnp.where(depth_row == pi.astype(F32), path, 0.0)
            take_s[s] = take.astype(BF)
            angle = (clen[r].astype(F32) + depth) * freq[...]
            at = slice(s * DRAFT, (s + 1) * DRAFT)
            cos_s[at, :] = jnp.cos(angle)
            sine = jnp.sin(angle)
            sin_s[at, :] = jnp.where(lane < HD // 2, -sine, sine)

    @pl.when(i < SLOTS)
    def _():
        s = i
        for p in range(DRAFT):
            raw[p * PITCH : p * PITCH + 64, :] = st[p * 64 : (p + 1) * 64, :].astype(F32)
        total = None
        for j in range(LT):
            x = hc_in[0, 0] * raw[pl.ds(j * NS, DRAFT, stride=PITCH), :]
            for m in range(1, NS):
                x = x + hc_in[0, m] * raw[pl.ds(j * NS + m, DRAFT, stride=PITCH), :]
            xbuf[:, j * 128 : (j + 1) * 128] = x
            total = x if total is None else total + x
        for j in range(LT):
            for n in range(NS):
                own[n, pl.ds(pl.multiple_of(s * Q, Q), Q), j * 128 : (j + 1) * 128] = raw[
                    pl.ds(place[1] * (Q * PITCH) + j * NS + n, Q, stride=PITCH), :
                ].astype(BF)
        center = jnp.sum(total, axis=-1, keepdims=True) * (1.0 / D)
        y = xbuf[...] - center
        spread = jnp.sum(y * y, axis=-1, keepdims=True) * (1.0 / D)
        normed[pl.ds(pl.multiple_of(s * DRAFT, DRAFT), DRAFT), :] = (
            y * lax.rsqrt(spread + 1e-05)
        ).astype(BF)

    def heads(g):
        arrive = loads(g)
        for c in arrive[:3]:
            c.wait()
        x = normed[...]
        q2 = mm(x, wq[g])
        k2 = mm(x, wk[g])
        v2 = mm(x, wv[g]).astype(BF)
        cosine = cos_s[...]
        sine = sin_s[...]
        col = lax.broadcasted_iota(jnp.int32, (DRAFT, CACHE), 1)
        for c in arrive[3:]:
            c.wait()
        kept = []
        for hh in range(2):
            cols = slice(hh * HD, (hh + 1) * HD)
            qh = q2[:, cols]
            kh = k2[:, cols]
            qh = (qh * cosine + pltpu.roll(qh, HD // 2, 1) * sine).astype(BF)
            kh = (kh * cosine + pltpu.roll(kh, HD // 2, 1) * sine).astype(BF)
            kept.append((cols, qh, kh, v2[:, cols]))
        todo = [(hh, s) for hh in range(2) for s in range(SLOTS)]
        for n, (hh, s) in enumerate(todo):
            cols, qh, kh, vh = kept[hh]
            at = slice(s * DRAFT, (s + 1) * DRAFT)
            to = slice(n * DRAFT, (n + 1) * DRAFT)
            length = clen[owner[base + s]]
            sc = mm_nt(qh[at], ck[g, s, :, cols]) * SCALE
            sc_s[to, :] = jnp.where(col < length, sc, -1e30)
            lo = mm_nt(qh[at], kh[at]) * SCALE
            lo_s[to, :] = jnp.where(above_s[s] > 0.5, lo, -1e30)
        for hh in range(2):
            to = slice(hh * 256, (hh + 1) * 256)
            sc = sc_s[to, :]
            lo = lo_s[to, :]
            top = jnp.maximum(
                jnp.max(sc, axis=-1, keepdims=True), jnp.max(lo, axis=-1, keepdims=True)
            )
            e1 = jnp.exp(sc - top)
            e2 = jnp.exp(lo - top)
            total = jnp.sum(e1, axis=-1, keepdims=True) + jnp.sum(e2, axis=-1, keepdims=True)
            inv = 1.0 / total
            w1_s[to, :] = (e1 * inv).astype(BF)
            w2_s[to, :] = (e2 * inv).astype(BF)
        for n, (hh, s) in enumerate(todo):
            cols, qh, kh, vh = kept[hh]
            at = slice(s * DRAFT, (s + 1) * DRAFT)
            to = slice(n * DRAFT, (n + 1) * DRAFT)
            o = mm(w1_s[to, :], cv[g, s, :, cols]) + mm(w2_s[to, :], vh[at])
            att[at, cols] = o.astype(BF)
            tk = take_s[s]
            h = g * 2 + hh
            kvs[s, pl.ds(h * 2, DRAFT, stride=8), :] = mm(tk, kh[at])
            kvs[s, pl.ds(h * 2 + 1, DRAFT, stride=8), :] = mm(tk, vh[at])
        part = mm(att[...], wo[g])
        if g == 0:
            acc[...] = part
        else:
            acc[...] = acc[...] + part
            for s in range(SLOTS):
                for k, out in enumerate((out0, out1, out2, out3)):
                    from_row = s * DRAFT + lax.rem(place[1] + k, 4) * Q
                    out[s * Q : (s + 1) * Q, :] = acc[
                        pl.ds(pl.multiple_of(from_row, Q), Q), :
                    ].astype(BF)
                kv_out[s * 512 : (s + 1) * 512, :] = kvs[s].astype(BF)

    @pl.when(i == SLOTS - 1)
    def _():
        heads(0)
        heads(1)


def front(place, owner, dlen, clen, pick, hc_in, parents, freq, st, wq, wk, wv, ck, cv, wo):
    smem = pl.BlockSpec(memory_space=pltpu.SMEM)
    vmem = pl.BlockSpec(memory_space=pltpu.VMEM)
    return pl.pallas_call(
        front_kernel,
        name="front",
        out_shape=(pltpu.VMEM((SLOTS * Q, D), BF),) * 4
        + (
            pltpu.VMEM((NS, SLOTS * Q, D), BF),
            jax.ShapeDtypeStruct((2048, 128), BF),
        ),
        grid_spec=pltpu.PrefetchScalarGridSpec(
            num_scalar_prefetch=5,
            grid=(SLOTS,),
            in_specs=[
                smem,
                pl.BlockSpec((DRAFT, 128), lambda i, *_: (0, 0)),
                pl.BlockSpec((1, HD), lambda i, *_: (0, 0)),
                pl.BlockSpec((4096, 128), lambda i, *_: (i, 0)),
            ]
            + [pl.BlockSpec(memory_space=pltpu.HBM)] * 6,
            out_specs=[vmem] * 5 + [pl.BlockSpec((2048, 128), lambda i, *_: (0, 0))],
            scratch_shapes=[
                pltpu.VMEM((DRAFT * PITCH, 128), F32),
                pltpu.VMEM((DRAFT, D), F32),
                pltpu.VMEM((SLOTS * DRAFT, D), BF),
                pltpu.VMEM((SLOTS, DRAFT, DRAFT), F32),
                pltpu.VMEM((SLOTS, DRAFT, DRAFT), BF),
                pltpu.VMEM((SLOTS * DRAFT, HD), F32),
                pltpu.VMEM((SLOTS * DRAFT, HD), F32),
                pltpu.VMEM((SLOTS * DRAFT, 256), BF),
                pltpu.VMEM((SLOTS * DRAFT, D), F32),
                pltpu.VMEM((SLOTS, 512, 128), F32),
                pltpu.VMEM((2, D, 256), BF),
                pltpu.VMEM((2, D, 256), BF),
                pltpu.VMEM((2, D, 256), BF),
                pltpu.VMEM((2, 256, D), BF),
                pltpu.VMEM((2, SLOTS, CACHE, 256), BF),
                pltpu.VMEM((2, SLOTS, CACHE, 256), BF),
                pltpu.VMEM((512, CACHE), F32),
                pltpu.VMEM((512, DRAFT), F32),
                pltpu.VMEM((512, CACHE), BF),
                pltpu.VMEM((512, DRAFT), BF),
                pltpu.SemaphoreType.DMA((2, 6)),
            ],
        ),
        compiler_params=pltpu.CompilerParams(vmem_limit_bytes=40 * 2**20),
    )(
        place,
        owner,
        dlen,
        clen,
        pick,
        hc_in,
        parents,
        freq,
        pltpu.with_memory_space_constraint(st, pltpu.HBM),
        *[pltpu.with_memory_space_constraint(x, pltpu.HBM) for x in (wq, wk, wv, wo, ck, cv)],
    )


def mid_kernel(hc_in, hc_res, hc_out, p0, p1, p2, p3, own, first, rows, xbuf):
    for s in range(SLOTS):
        at = slice(s * Q, (s + 1) * Q)
        total = None
        for j in range(LT):
            lanes = slice(j * 128, (j + 1) * 128)
            attn = p0[at, lanes].astype(F32)
            for p in (p1, p2, p3):
                attn = attn + p[at, lanes].astype(F32)
            mine = [own[n, at, lanes].astype(F32) for n in range(NS)]
            x = None
            for m in range(NS):
                c = hc_out[0, m] * attn
                for n in range(NS):
                    c = c + hc_res[0, n, m] * mine[n]
                c = c.astype(BF)
                first[m, at, lanes] = c
                t = hc_in[1, m] * c.astype(F32)
                x = t if x is None else x + t
            xbuf[at, lanes] = x
            total = x if total is None else total + x
        center = jnp.sum(total, axis=-1, keepdims=True) * (1.0 / D)
        y = xbuf[at, :] - center
        spread = jnp.sum(y * y, axis=-1, keepdims=True) * (1.0 / D)
        rows[at, :] = (y * lax.rsqrt(spread + 1e-05)).astype(BF)


def mid(hc_in, hc_res, hc_out, parts, own):
    smem = pl.BlockSpec(memory_space=pltpu.SMEM)
    vmem = pl.BlockSpec(memory_space=pltpu.VMEM)
    return pl.pallas_call(
        mid_kernel,
        name="mid",
        out_shape=(pltpu.VMEM((NS, SLOTS * Q, D), BF), pltpu.VMEM((SLOTS * Q, D), BF)),
        in_specs=[smem] * 3 + [vmem] * 5,
        out_specs=(vmem, vmem),
        scratch_shapes=[pltpu.VMEM((SLOTS * Q, D), F32)],
        compiler_params=pltpu.CompilerParams(vmem_limit_bytes=8 * 2**20),
    )(hc_in, hc_res, hc_out, *[near(p) for p in parts], near(own))


def last_kernel(place, owner, dlen, hc_res, hc_out, first, *refs):
    parts, out, raw = refs[:MEMBERS], refs[MEMBERS], refs[MEMBERS + 1]
    spot = place[1] * Q + lax.broadcasted_iota(jnp.int32, (Q, 128), 0)
    for s in range(SLOTS):
        at = slice(s * Q, (s + 1) * Q)
        alive = spot < dlen[owner[place[0] * SLOTS + s]]
        for j in range(LT):
            lanes = slice(j * 128, (j + 1) * 128)
            mlp = parts[0][at, lanes].astype(F32)
            for p in parts[1:]:
                mlp = mlp + p[at, lanes].astype(F32)
            f = [first[n, at, lanes].astype(F32) for n in range(NS)]
            for m in range(NS):
                c = hc_out[1, m] * mlp
                for n in range(NS):
                    c = c + hc_res[1, n, m] * f[n]
                raw[pl.ds(j * NS + m, Q, stride=PITCH), :] = jnp.where(alive, c, 0.0)
        for p in range(Q):
            out[(s * Q + p) * 64 : (s * Q + p + 1) * 64, :] = raw[
                p * PITCH : p * PITCH + 64, :
            ].astype(BF)


def last(place, owner, dlen, hc_res, hc_out, first, parts):
    smem = pl.BlockSpec(memory_space=pltpu.SMEM)
    vmem = pl.BlockSpec(memory_space=pltpu.VMEM)
    return pl.pallas_call(
        last_kernel,
        name="last",
        out_shape=jax.ShapeDtypeStruct((SLOTS * 1024, 128), BF),
        in_specs=[smem] * 5 + [vmem] * (1 + MEMBERS),
        out_specs=vmem,
        scratch_shapes=[pltpu.VMEM((Q * PITCH, 128), F32)],
        compiler_params=pltpu.CompilerParams(vmem_limit_bytes=8 * 2**20),
    )(place, owner, dlen, hc_res, hc_out, near(first), *[near(p) for p in parts])


def pack_kernel(g, u, d, one, two, sems):
    ins = []
    for k, w in enumerate((one, two)):
        part = pl.ds(k * 128, 128)
        ins.append(
            pltpu.make_async_copy(g.at[:, part], w.at[pl.ds(0, D), pl.ds(0, 128)], sems.at[k, 0])
        )
        ins.append(
            pltpu.make_async_copy(u.at[:, part], w.at[pl.ds(0, D), pl.ds(128, 128)], sems.at[k, 1])
        )
        for c in range(8):
            ins.append(
                pltpu.make_async_copy(
                    d.at[part, pl.ds(256 * c, 256)],
                    w.at[pl.ds(D + 128 * c, 128), :],
                    sems.at[k, 2 + c],
                )
            )
    for c in ins:
        c.start()
    for c in ins:
        c.wait()


def pack(g, u, d):
    hbm = pl.BlockSpec(memory_space=pltpu.HBM)
    vmem = pl.BlockSpec(memory_space=pltpu.VMEM)
    return pl.pallas_call(
        pack_kernel,
        name="pack",
        out_shape=(pltpu.VMEM((PACKED, 256), BF),) * 2,
        in_specs=[hbm] * 3,
        out_specs=(vmem, vmem),
        scratch_shapes=[pltpu.SemaphoreType.DMA((2, 10))],
        compiler_params=pltpu.CompilerParams(vmem_limit_bytes=8 * 2**20),
    )(*[pltpu.with_memory_space_constraint(x, pltpu.HBM) for x in (g, u, d)])


def ffn_kernel(n, *refs):
    xs, ws, ys = refs[:n], refs[n : n + BLOCKS], refs[n + BLOCKS : 2 * n + BLOCKS]
    cat, inner = refs[2 * n + BLOCKS :]
    rows = SLOTS * Q
    for k, x in enumerate(xs):
        cat[k * rows : (k + 1) * rows, :] = x[...]
    step = CH * rows
    spans = [(o, min(o + step, n * rows)) for o in range(0, n * rows, step)]
    for lo, hi in spans:
        for k, w in enumerate(ws):
            both = mm(cat[lo:hi, :], w[:D, :])
            gate = both[:, :128]
            inner[lo:hi, k * 128 : (k + 1) * 128] = (
                gate / (1.0 + jnp.exp(-gate)) * both[:, 128:]
            ).astype(BF)
        for c in range(8):
            at = D + 128 * c
            down = jnp.concatenate([w[at : at + 128, :] for w in ws], axis=0)
            t = mm(inner[lo:hi, :], down).astype(BF)
            for k in range(lo // rows, hi // rows):
                ys[k][:, 256 * c : 256 * (c + 1)] = t[k * rows - lo : (k + 1) * rows - lo]


def ffn(xs, weights):
    n = len(xs)
    vmem = pl.BlockSpec(memory_space=pltpu.VMEM)
    rows = n * SLOTS * Q
    return pl.pallas_call(
        functools.partial(ffn_kernel, n),
        name="ffn",
        out_shape=tuple(pltpu.VMEM((SLOTS * Q, D), BF) for _ in xs),
        in_specs=[vmem] * (n + BLOCKS),
        out_specs=tuple([vmem] * n),
        scratch_shapes=[
            pltpu.VMEM((rows, D), BF),
            pltpu.VMEM((rows, 128 * BLOCKS), BF),
        ],
        cost_estimate=pl.CostEstimate(
            flops=rows * D * 1024 * 6, transcendentals=rows * 1024, bytes_accessed=rows * D * 4
        ),
        compiler_params=pltpu.CompilerParams(vmem_limit_bytes=24 * 2**20),
    )(*[near(x) for x in xs], *[near(w) for w in weights])


def pairs(move):
    out = []
    for x in range(4):
        for z in range(4):
            for c in range(2):
                tx, tz, tc = move(x, z, c)
                out.append((x * 8 + z * 2 + c, (tx % 4) * 8 + (tz % 4) * 2 + tc))
    return out


def send(v, move):
    return lax.ppermute(v, "req", pairs(move))


def shift(v, dx, dz):
    return send(v, lambda x, z, c: (x + dx, z + dz, c))


def other_core(v):
    return send(v, lambda x, z, c: (x, z, 1 - c))


def body(
    streams,
    w_query,
    w_key,
    w_value,
    w_output,
    w_gate,
    w_up,
    w_down,
    cache_keys,
    cache_values,
    hc_in,
    hc_res,
    hc_out,
    parents,
    draft_len,
    cache_len,
    accept_pick,
    slot_owner,
):
    place = jnp.stack([lax.axis_index("req"), lax.axis_index("head")]).astype(jnp.int32)
    half = np.arange(64, dtype=np.float64)
    freq = np.power(10000.0, -(half * 2.0 / HD)).astype(np.float32)
    freq = jnp.asarray(np.concatenate([freq, freq])[None, :])
    st = streams.reshape(SLOTS, DRAFT, NS, LT, 128).transpose(0, 1, 3, 2, 4).reshape(-1, 128)
    one, two = pack(w_gate, w_up, w_down)
    one_z = send(one, lambda x, z, c: (x, z ^ 1, c))
    two_x = send(two, lambda x, z, c: (x ^ 1, z, c))
    one_c, two_c = other_core(one), other_core(two)
    *out, own, kv = front(
        place,
        slot_owner,
        draft_len,
        cache_len,
        accept_pick,
        hc_in,
        parents.T,
        freq,
        st,
        w_query,
        w_key,
        w_value,
        cache_keys,
        cache_values,
        w_output,
    )
    turn = lambda v, k: lax.ppermute(v, "head", [(y, (y + k) % 4) for y in range(4)])
    out, one_c, two_c = lax.optimization_barrier((out, one_c, two_c))
    p1 = turn(out[1], 1)
    p3 = turn(out[3], 3)
    p2 = turn(out[2], 2)
    p1, p2, p3, one_z, two_x = lax.optimization_barrier((p1, p2, p3, one_z, two_x))
    weights = (one, two, one_c, two_c, one_z, two_x, other_core(one_z), other_core(two_x))
    first, rows = mid(hc_in, hc_res, hc_out, [out[0], p1, p2, p3], own)
    rows, weights = lax.optimization_barrier((rows, weights))
    pieces = [rows] + [shift(rows, dx, dz) for dx, dz in OFFSETS]
    sums = ffn(pieces, weights)
    back = [sums[0]] + [shift(t, -dx, -dz) for t, (dx, dz) in zip(sums[1:], OFFSETS)]
    final = last(place, slot_owner, draft_len, hc_res, hc_out, first, back)
    new_streams = (
        final.reshape(SLOTS, Q, LT, NS, 128).transpose(0, 1, 3, 2, 4).reshape(SLOTS, Q, NS, D)
    )
    accepted_kv = (
        kv.reshape(SLOTS, DRAFT, 4, 2, 128).transpose(0, 1, 3, 2, 4).reshape(SLOTS, DRAFT, 2, 512)
    )
    return (new_streams, accepted_kv)


def solution(mesh):
    placed = (
        P("req", None, None, None),
        P(None, "head"),
        P(None, "head"),
        P(None, "head"),
        P("head", None),
        P(None, "req"),
        P(None, "req"),
        P("req", None),
        P("req", None, "head"),
        P("req", None, "head"),
        P(),
        P(),
        P(),
        P(),
        P(),
        P(),
        P(),
        P(),
    )
    return jax.shard_map(
        body,
        mesh=mesh,
        in_specs=placed,
        out_specs=(P("req", "head", None, None), P("req", None, None, "head")),
        check_vma=False,
    )
```

```python
import functools

import jax
import jax.numpy as jnp
import numpy as np
from jax import lax
from jax.experimental import pallas as pl
from jax.experimental.pallas import tpu as pltpu
from jax.sharding import PartitionSpec as P

HD = 128
SLOTS = 4
DRAFT = 64
CACHE = 1024
D = 2048
NS = 4
LT = D // 128
Q = 16
SCALE = HD ** (-0.5)
BF = jnp.bfloat16
F32 = jnp.float32
BLOCKS = 8
PITCH = 72
PACKED = 3072
OFFSETS = ((1, 1), (-1, -1), (1, -1), (-1, 1), (2, 0), (0, 2), (2, 2))
MEMBERS = len(OFFSETS) + 1
FIRST = 4
CH = 4
NT = (((1,), (1,)), ((), ()))


def near(x):
    return pltpu.with_memory_space_constraint(x, pltpu.VMEM)


def mm(a, b):
    return jnp.dot(a, b, preferred_element_type=F32)


def mm_nt(a, b):
    return lax.dot_general(a, b, NT, preferred_element_type=F32)


def normalize(x):
    center = jnp.sum(x, axis=-1, keepdims=True) * (1.0 / D)
    y = x - center
    spread = jnp.sum(y * y, axis=-1, keepdims=True) * (1.0 / D)
    return y * lax.rsqrt(spread + 1e-05)


def front_kernel(
    place,
    owner,
    dlen,
    clen,
    pick,
    hc_in,
    parents,
    freq,
    st,
    wq_h,
    wk_h,
    wv_h,
    wo_h,
    ck_h,
    cv_h,
    out0,
    out1,
    out2,
    out3,
    own,
    kv_out,
    raw,
    xbuf,
    normed,
    above_s,
    take_s,
    cos_s,
    sin_s,
    att,
    acc,
    kvs,
    wq,
    wk,
    wv,
    wo,
    ck,
    cv,
    sc_s,
    lo_s,
    w1_s,
    w2_s,
    sems,
):
    i = pl.program_id(0)
    base = place[0] * SLOTS

    def loads(g):
        cols = pl.ds(g * 256, 256)
        return (
            pltpu.make_async_copy(wq_h.at[:, cols], wq.at[g], sems.at[g, 0]),
            pltpu.make_async_copy(wk_h.at[:, cols], wk.at[g], sems.at[g, 1]),
            pltpu.make_async_copy(wv_h.at[:, cols], wv.at[g], sems.at[g, 2]),
            pltpu.make_async_copy(ck_h.at[:, :, cols], ck.at[g], sems.at[g, 3]),
            pltpu.make_async_copy(cv_h.at[:, :, cols], cv.at[g], sems.at[g, 4]),
            pltpu.make_async_copy(wo_h.at[cols, :], wo.at[g], sems.at[g, 5]),
        )

    @pl.when(i == 0)
    def _():
        for c in loads(0):
            c.start()

    @pl.when(i == SLOTS - 1)
    def _():
        for c in loads(1):
            c.start()

    @pl.when(i == 0)
    def _():
        pi = lax.broadcasted_iota(jnp.int32, (DRAFT, DRAFT), 0)
        qi = lax.broadcasted_iota(jnp.int32, (DRAFT, DRAFT), 1)
        eye = (qi == pi).astype(F32)
        who = lax.broadcasted_iota(jnp.int32, (DRAFT, 128), 1)
        lane = lax.broadcasted_iota(jnp.int32, (DRAFT, HD), 1)
        ones = jnp.ones((8, DRAFT), BF)
        ups = []
        for s in range(SLOTS):
            r = owner[base + s]
            par = jnp.sum(jnp.where(who == r, parents[...], 0), axis=1, keepdims=True)
            ups.append(jnp.where(par == qi, 1.0, eye))
        for rounds in range(6):
            nxt = []
            for up in ups:
                b = up.astype(BF)
                nxt.append(jnp.minimum(mm(b, b), 1.0))
            ups = nxt
        for s in range(SLOTS):
            r = owner[base + s]
            above = ups[s]
            above_s[s] = above
            depth_row = mm_nt(ones, above.astype(BF))[0:1] - 1.0
            depth = jnp.sum(above, axis=1, keepdims=True) - 1.0
            a = jnp.minimum(pick[r], dlen[r] - 1)
            path = above_s[s, pl.ds(a, 1), :]
            take = jnp.where(depth_row == pi.astype(F32), path, 0.0)
            take_s[s] = take.astype(BF)
            angle = (clen[r].astype(F32) + depth) * freq[...]
            at = slice(s * DRAFT, (s + 1) * DRAFT)
            cos_s[at, :] = jnp.cos(angle)
            sine = jnp.sin(angle)
            sin_s[at, :] = jnp.where(lane < HD // 2, -sine, sine)

    @pl.when(i < SLOTS)
    def _():
        s = i
        for p in range(DRAFT):
            raw[p * PITCH : p * PITCH + 64, :] = st[p * 64 : (p + 1) * 64, :].astype(F32)
        total = None
        for j in range(LT):
            x = hc_in[0, 0] * raw[pl.ds(j * NS, DRAFT, stride=PITCH), :]
            for m in range(1, NS):
                x = x + hc_in[0, m] * raw[pl.ds(j * NS + m, DRAFT, stride=PITCH), :]
            xbuf[:, j * 128 : (j + 1) * 128] = x
            total = x if total is None else total + x
        for j in range(LT):
            for n in range(NS):
                own[n, pl.ds(pl.multiple_of(s * Q, Q), Q), j * 128 : (j + 1) * 128] = raw[
                    pl.ds(place[1] * (Q * PITCH) + j * NS + n, Q, stride=PITCH), :
                ].astype(BF)
        center = jnp.sum(total, axis=-1, keepdims=True) * (1.0 / D)
        y = xbuf[...] - center
        spread = jnp.sum(y * y, axis=-1, keepdims=True) * (1.0 / D)
        normed[pl.ds(pl.multiple_of(s * DRAFT, DRAFT), DRAFT), :] = (
            y * lax.rsqrt(spread + 1e-05)
        ).astype(BF)

    def heads(g):
        arrive = loads(g)
        for c in arrive[:3]:
            c.wait()
        x = normed[...]
        q2 = mm(x, wq[g])
        k2 = mm(x, wk[g])
        v2 = mm(x, wv[g]).astype(BF)
        cosine = cos_s[...]
        sine = sin_s[...]
        col = lax.broadcasted_iota(jnp.int32, (DRAFT, CACHE), 1)
        for c in arrive[3:]:
            c.wait()
        kept = []
        for hh in range(2):
            cols = slice(hh * HD, (hh + 1) * HD)
            qh = q2[:, cols]
            kh = k2[:, cols]
            qh = (qh * cosine + pltpu.roll(qh, HD // 2, 1) * sine).astype(BF)
            kh = (kh * cosine + pltpu.roll(kh, HD // 2, 1) * sine).astype(BF)
            kept.append((cols, qh, kh, v2[:, cols]))
        todo = [(hh, s) for hh in range(2) for s in range(SLOTS)]
        for n, (hh, s) in enumerate(todo):
            cols, qh, kh, vh = kept[hh]
            at = slice(s * DRAFT, (s + 1) * DRAFT)
            to = slice(n * DRAFT, (n + 1) * DRAFT)
            length = clen[owner[base + s]]
            sc = mm_nt(qh[at], ck[g, s, :, cols]) * SCALE
            sc_s[to, :] = jnp.where(col < length, sc, -1e30)
            lo = mm_nt(qh[at], kh[at]) * SCALE
            lo_s[to, :] = jnp.where(above_s[s] > 0.5, lo, -1e30)
        for hh in range(2):
            to = slice(hh * 256, (hh + 1) * 256)
            sc = sc_s[to, :]
            lo = lo_s[to, :]
            top = jnp.maximum(
                jnp.max(sc, axis=-1, keepdims=True), jnp.max(lo, axis=-1, keepdims=True)
            )
            e1 = jnp.exp(sc - top)
            e2 = jnp.exp(lo - top)
            total = jnp.sum(e1, axis=-1, keepdims=True) + jnp.sum(e2, axis=-1, keepdims=True)
            inv = 1.0 / total
            w1_s[to, :] = (e1 * inv).astype(BF)
            w2_s[to, :] = (e2 * inv).astype(BF)
        for n, (hh, s) in enumerate(todo):
            cols, qh, kh, vh = kept[hh]
            at = slice(s * DRAFT, (s + 1) * DRAFT)
            to = slice(n * DRAFT, (n + 1) * DRAFT)
            o = mm(w1_s[to, :], cv[g, s, :, cols]) + mm(w2_s[to, :], vh[at])
            att[at, cols] = o.astype(BF)
            tk = take_s[s]
            h = g * 2 + hh
            kvs[s, pl.ds(h * 2, DRAFT, stride=8), :] = mm(tk, kh[at])
            kvs[s, pl.ds(h * 2 + 1, DRAFT, stride=8), :] = mm(tk, vh[at])
        part = mm(att[...], wo[g])
        if g == 0:
            acc[...] = part
        else:
            acc[...] = acc[...] + part
            for s in range(SLOTS):
                for k, out in enumerate((out0, out1, out2, out3)):
                    from_row = s * DRAFT + lax.rem(place[1] + k, 4) * Q
                    out[s * Q : (s + 1) * Q, :] = acc[
                        pl.ds(pl.multiple_of(from_row, Q), Q), :
                    ].astype(BF)
                kv_out[s * 512 : (s + 1) * 512, :] = kvs[s].astype(BF)

    @pl.when(i == SLOTS - 1)
    def _():
        heads(0)
        heads(1)


def front(place, owner, dlen, clen, pick, hc_in, parents, freq, st, wq, wk, wv, ck, cv, wo):
    smem = pl.BlockSpec(memory_space=pltpu.SMEM)
    vmem = pl.BlockSpec(memory_space=pltpu.VMEM)
    return pl.pallas_call(
        front_kernel,
        name="front",
        out_shape=(pltpu.VMEM((SLOTS * Q, D), BF),) * 4
        + (
            pltpu.VMEM((NS, SLOTS * Q, D), BF),
            jax.ShapeDtypeStruct((2048, 128), BF),
        ),
        grid_spec=pltpu.PrefetchScalarGridSpec(
            num_scalar_prefetch=5,
            grid=(SLOTS,),
            in_specs=[
                smem,
                pl.BlockSpec((DRAFT, 128), lambda i, *_: (0, 0)),
                pl.BlockSpec((1, HD), lambda i, *_: (0, 0)),
                pl.BlockSpec((4096, 128), lambda i, *_: (i, 0)),
            ]
            + [pl.BlockSpec(memory_space=pltpu.HBM)] * 6,
            out_specs=[vmem] * 5 + [pl.BlockSpec((2048, 128), lambda i, *_: (0, 0))],
            scratch_shapes=[
                pltpu.VMEM((DRAFT * PITCH, 128), F32),
                pltpu.VMEM((DRAFT, D), F32),
                pltpu.VMEM((SLOTS * DRAFT, D), BF),
                pltpu.VMEM((SLOTS, DRAFT, DRAFT), F32),
                pltpu.VMEM((SLOTS, DRAFT, DRAFT), BF),
                pltpu.VMEM((SLOTS * DRAFT, HD), F32),
                pltpu.VMEM((SLOTS * DRAFT, HD), F32),
                pltpu.VMEM((SLOTS * DRAFT, 256), BF),
                pltpu.VMEM((SLOTS * DRAFT, D), F32),
                pltpu.VMEM((SLOTS, 512, 128), F32),
                pltpu.VMEM((2, D, 256), BF),
                pltpu.VMEM((2, D, 256), BF),
                pltpu.VMEM((2, D, 256), BF),
                pltpu.VMEM((2, 256, D), BF),
                pltpu.VMEM((2, SLOTS, CACHE, 256), BF),
                pltpu.VMEM((2, SLOTS, CACHE, 256), BF),
                pltpu.VMEM((512, CACHE), F32),
                pltpu.VMEM((512, DRAFT), F32),
                pltpu.VMEM((512, CACHE), BF),
                pltpu.VMEM((512, DRAFT), BF),
                pltpu.SemaphoreType.DMA((2, 6)),
            ],
        ),
        compiler_params=pltpu.CompilerParams(vmem_limit_bytes=40 * 2**20),
    )(
        place,
        owner,
        dlen,
        clen,
        pick,
        hc_in,
        parents,
        freq,
        pltpu.with_memory_space_constraint(st, pltpu.HBM),
        *[pltpu.with_memory_space_constraint(x, pltpu.HBM) for x in (wq, wk, wv, wo, ck, cv)],
    )


def mid_kernel(hc_in, hc_res, hc_out, p0, p1, p2, p3, own, first, rows, xbuf):
    for s in range(SLOTS):
        at = slice(s * Q, (s + 1) * Q)
        total = None
        for j in range(LT):
            lanes = slice(j * 128, (j + 1) * 128)
            attn = p0[at, lanes].astype(F32)
            for p in (p1, p2, p3):
                attn = attn + p[at, lanes].astype(F32)
            mine = [own[n, at, lanes].astype(F32) for n in range(NS)]
            x = None
            for m in range(NS):
                c = hc_out[0, m] * attn
                for n in range(NS):
                    c = c + hc_res[0, n, m] * mine[n]
                c = c.astype(BF)
                first[m, at, lanes] = c
                t = hc_in[1, m] * c.astype(F32)
                x = t if x is None else x + t
            xbuf[at, lanes] = x
            total = x if total is None else total + x
        center = jnp.sum(total, axis=-1, keepdims=True) * (1.0 / D)
        y = xbuf[at, :] - center
        spread = jnp.sum(y * y, axis=-1, keepdims=True) * (1.0 / D)
        rows[at, :] = (y * lax.rsqrt(spread + 1e-05)).astype(BF)


def mid(hc_in, hc_res, hc_out, parts, own):
    smem = pl.BlockSpec(memory_space=pltpu.SMEM)
    vmem = pl.BlockSpec(memory_space=pltpu.VMEM)
    return pl.pallas_call(
        mid_kernel,
        name="mid",
        out_shape=(pltpu.VMEM((NS, SLOTS * Q, D), BF), pltpu.VMEM((SLOTS * Q, D), BF)),
        in_specs=[smem] * 3 + [vmem] * 5,
        out_specs=(vmem, vmem),
        scratch_shapes=[pltpu.VMEM((SLOTS * Q, D), F32)],
        compiler_params=pltpu.CompilerParams(vmem_limit_bytes=8 * 2**20),
    )(hc_in, hc_res, hc_out, *[near(p) for p in parts], near(own))


def last_kernel(place, owner, dlen, hc_res, hc_out, first, *refs):
    parts, out, raw = refs[:MEMBERS], refs[MEMBERS], refs[MEMBERS + 1]
    spot = place[1] * Q + lax.broadcasted_iota(jnp.int32, (Q, 128), 0)
    for s in range(SLOTS):
        at = slice(s * Q, (s + 1) * Q)
        alive = spot < dlen[owner[place[0] * SLOTS + s]]
        for j in range(LT):
            lanes = slice(j * 128, (j + 1) * 128)
            mlp = parts[0][at, lanes].astype(F32)
            for p in parts[1:]:
                mlp = mlp + p[at, lanes].astype(F32)
            f = [first[n, at, lanes].astype(F32) for n in range(NS)]
            for m in range(NS):
                c = hc_out[1, m] * mlp
                for n in range(NS):
                    c = c + hc_res[1, n, m] * f[n]
                raw[pl.ds(j * NS + m, Q, stride=PITCH), :] = jnp.where(alive, c, 0.0)
        for p in range(Q):
            out[(s * Q + p) * 64 : (s * Q + p + 1) * 64, :] = raw[
                p * PITCH : p * PITCH + 64, :
            ].astype(BF)


def last(place, owner, dlen, hc_res, hc_out, first, parts):
    smem = pl.BlockSpec(memory_space=pltpu.SMEM)
    vmem = pl.BlockSpec(memory_space=pltpu.VMEM)
    return pl.pallas_call(
        last_kernel,
        name="last",
        out_shape=jax.ShapeDtypeStruct((SLOTS * 1024, 128), BF),
        in_specs=[smem] * 5 + [vmem] * (1 + MEMBERS),
        out_specs=vmem,
        scratch_shapes=[pltpu.VMEM((Q * PITCH, 128), F32)],
        compiler_params=pltpu.CompilerParams(vmem_limit_bytes=8 * 2**20),
    )(place, owner, dlen, hc_res, hc_out, near(first), *[near(p) for p in parts])


def pack_kernel(g, u, d, one, two, sems):
    ins = []
    for k, w in enumerate((one, two)):
        part = pl.ds(k * 128, 128)
        ins.append(
            pltpu.make_async_copy(g.at[:, part], w.at[pl.ds(0, D), pl.ds(0, 128)], sems.at[k, 0])
        )
        ins.append(
            pltpu.make_async_copy(u.at[:, part], w.at[pl.ds(0, D), pl.ds(128, 128)], sems.at[k, 1])
        )
        for c in range(8):
            ins.append(
                pltpu.make_async_copy(
                    d.at[part, pl.ds(256 * c, 256)],
                    w.at[pl.ds(D + 128 * c, 128), :],
                    sems.at[k, 2 + c],
                )
            )
    for c in ins:
        c.start()
    for c in ins:
        c.wait()


def pack(g, u, d):
    hbm = pl.BlockSpec(memory_space=pltpu.HBM)
    vmem = pl.BlockSpec(memory_space=pltpu.VMEM)
    return pl.pallas_call(
        pack_kernel,
        name="pack",
        out_shape=(pltpu.VMEM((PACKED, 256), BF),) * 2,
        in_specs=[hbm] * 3,
        out_specs=(vmem, vmem),
        scratch_shapes=[pltpu.SemaphoreType.DMA((2, 10))],
        compiler_params=pltpu.CompilerParams(vmem_limit_bytes=8 * 2**20),
    )(*[pltpu.with_memory_space_constraint(x, pltpu.HBM) for x in (g, u, d)])


def ffn_kernel(n, *refs):
    xs, ws, ys = refs[:n], refs[n : n + BLOCKS], refs[n + BLOCKS : 2 * n + BLOCKS]
    cat, inner = refs[2 * n + BLOCKS :]
    rows = SLOTS * Q
    for k, x in enumerate(xs):
        cat[k * rows : (k + 1) * rows, :] = x[...]
    step = CH * rows
    spans = [(o, min(o + step, n * rows)) for o in range(0, n * rows, step)]
    for lo, hi in spans:
        for k, w in enumerate(ws):
            both = mm(cat[lo:hi, :], w[:D, :])
            gate = both[:, :128]
            inner[lo:hi, k * 128 : (k + 1) * 128] = (
                gate / (1.0 + jnp.exp(-gate)) * both[:, 128:]
            ).astype(BF)
        for c in range(8):
            at = D + 128 * c
            down = jnp.concatenate([w[at : at + 128, :] for w in ws], axis=0)
            t = mm(inner[lo:hi, :], down).astype(BF)
            for k in range(lo // rows, hi // rows):
                ys[k][:, 256 * c : 256 * (c + 1)] = t[k * rows - lo : (k + 1) * rows - lo]


def ffn(xs, weights):
    n = len(xs)
    vmem = pl.BlockSpec(memory_space=pltpu.VMEM)
    rows = n * SLOTS * Q
    return pl.pallas_call(
        functools.partial(ffn_kernel, n),
        name="ffn",
        out_shape=tuple(pltpu.VMEM((SLOTS * Q, D), BF) for _ in xs),
        in_specs=[vmem] * (n + BLOCKS),
        out_specs=tuple([vmem] * n),
        scratch_shapes=[
            pltpu.VMEM((rows, D), BF),
            pltpu.VMEM((rows, 128 * BLOCKS), BF),
        ],
        cost_estimate=pl.CostEstimate(
            flops=rows * D * 1024 * 6, transcendentals=rows * 1024, bytes_accessed=rows * D * 4
        ),
        compiler_params=pltpu.CompilerParams(vmem_limit_bytes=24 * 2**20),
    )(*[near(x) for x in xs], *[near(w) for w in weights])


def pairs(move):
    out = []
    for x in range(4):
        for z in range(4):
            for c in range(2):
                tx, tz, tc = move(x, z, c)
                out.append((x * 8 + z * 2 + c, (tx % 4) * 8 + (tz % 4) * 2 + tc))
    return out


def send(v, move):
    return lax.ppermute(v, "req", pairs(move))


def shift(v, dx, dz):
    return send(v, lambda x, z, c: (x + dx, z + dz, c))


def other_core(v):
    return send(v, lambda x, z, c: (x, z, 1 - c))


def body(
    streams,
    w_query,
    w_key,
    w_value,
    w_output,
    w_gate,
    w_up,
    w_down,
    cache_keys,
    cache_values,
    hc_in,
    hc_res,
    hc_out,
    parents,
    draft_len,
    cache_len,
    accept_pick,
    slot_owner,
):
    place = jnp.stack([lax.axis_index("req"), lax.axis_index("head")]).astype(jnp.int32)
    half = np.arange(64, dtype=np.float64)
    freq = np.power(10000.0, -(half * 2.0 / HD)).astype(np.float32)
    freq = jnp.asarray(np.concatenate([freq, freq])[None, :])
    st = streams.reshape(SLOTS, DRAFT, NS, LT, 128).transpose(0, 1, 3, 2, 4).reshape(-1, 128)
    one, two = pack(w_gate, w_up, w_down)
    one_z = send(one, lambda x, z, c: (x, z + 2 * c - 1, c))
    two_x = send(two, lambda x, z, c: (x + 2 * c - 1, z, c))
    one_c, two_c = other_core(one), other_core(two)
    *out, own, kv = front(
        place,
        slot_owner,
        draft_len,
        cache_len,
        accept_pick,
        hc_in,
        parents.T,
        freq,
        st,
        w_query,
        w_key,
        w_value,
        cache_keys,
        cache_values,
        w_output,
    )
    turn = lambda v, k: lax.ppermute(v, "head", [(y, (y + k) % 4) for y in range(4)])
    out, one_c, two_c, one_z, two_x = lax.optimization_barrier((out, one_c, two_c, one_z, two_x))
    one_zc, two_xc = other_core(one_z), other_core(two_x)
    p1 = turn(out[1], 1)
    p3 = turn(out[3], 3)
    p2 = turn(out[2], 2)
    weights = (one, two, one_c, two_c, one_z, two_x, one_zc, two_xc)
    first, rows = mid(hc_in, hc_res, hc_out, [out[0], p1, p2, p3], own)
    rows, weights = lax.optimization_barrier((rows, weights))
    pieces = [rows] + [shift(rows, dx, dz) for dx, dz in OFFSETS]
    sums = ffn(pieces[:FIRST], weights) + ffn(pieces[FIRST:], weights)
    back = [sums[0]] + [shift(t, -dx, -dz) for t, (dx, dz) in zip(sums[1:], OFFSETS)]
    final = last(place, slot_owner, draft_len, hc_res, hc_out, first, back)
    new_streams = (
        final.reshape(SLOTS, Q, LT, NS, 128).transpose(0, 1, 3, 2, 4).reshape(SLOTS, Q, NS, D)
    )
    accepted_kv = (
        kv.reshape(SLOTS, DRAFT, 4, 2, 128).transpose(0, 1, 3, 2, 4).reshape(SLOTS, DRAFT, 2, 512)
    )
    return (new_streams, accepted_kv)


def solution(mesh):
    placed = (
        P("req", None, None, None),
        P(None, "head"),
        P(None, "head"),
        P(None, "head"),
        P("head", None),
        P(None, "req"),
        P(None, "req"),
        P("req", None),
        P("req", None, "head"),
        P("req", None, "head"),
        P(),
        P(),
        P(),
        P(),
        P(),
        P(),
        P(),
        P(),
    )
    return jax.shard_map(
        body,
        mesh=mesh,
        in_specs=placed,
        out_specs=(P("req", "head", None, None), P("req", None, None, "head")),
        check_vma=False,
    )
```

```python
import functools

import jax
import jax.numpy as jnp
import numpy as np
from jax import lax
from jax.experimental import pallas as pl
from jax.experimental.pallas import tpu as pltpu
from jax.sharding import PartitionSpec as P

HD = 128
SLOTS = 4
DRAFT = 64
CACHE = 1024
D = 2048
NS = 4
LT = D // 128
Q = 16
SCALE = HD ** (-0.5)
BF = jnp.bfloat16
F32 = jnp.float32
BLOCKS = 8
PITCH = 72
PACKED = 3072
OFFSETS = ((1, 1), (-1, -1), (1, -1), (-1, 1), (2, 0), (0, 2), (2, 2))
MEMBERS = len(OFFSETS) + 1
FIRST = 4
CH = 4
NT = (((1,), (1,)), ((), ()))


def near(x):
    return pltpu.with_memory_space_constraint(x, pltpu.VMEM)


def mm(a, b):
    return jnp.dot(a, b, preferred_element_type=F32)


def mm_nt(a, b):
    return lax.dot_general(a, b, NT, preferred_element_type=F32)


def normalize(x):
    center = jnp.sum(x, axis=-1, keepdims=True) * (1.0 / D)
    y = x - center
    spread = jnp.sum(y * y, axis=-1, keepdims=True) * (1.0 / D)
    return y * lax.rsqrt(spread + 1e-05)


def front_kernel(
    place,
    owner,
    dlen,
    clen,
    pick,
    hc_in,
    parents,
    freq,
    st,
    wq_h,
    wk_h,
    wv_h,
    wo_h,
    ck_h,
    cv_h,
    out0,
    out1,
    out2,
    out3,
    own,
    kv_out,
    raw,
    xbuf,
    normed,
    above_s,
    take_s,
    cos_s,
    sin_s,
    att,
    acc,
    kvs,
    wq,
    wk,
    wv,
    wo,
    ck,
    cv,
    sc_s,
    lo_s,
    w1_s,
    w2_s,
    sems,
):
    i = pl.program_id(0)
    base = place[0] * SLOTS

    def loads(g):
        cols = pl.ds(g * 256, 256)
        return (
            pltpu.make_async_copy(wq_h.at[:, cols], wq.at[g], sems.at[g, 0]),
            pltpu.make_async_copy(wk_h.at[:, cols], wk.at[g], sems.at[g, 1]),
            pltpu.make_async_copy(wv_h.at[:, cols], wv.at[g], sems.at[g, 2]),
            pltpu.make_async_copy(ck_h.at[:, :, cols], ck.at[g], sems.at[g, 3]),
            pltpu.make_async_copy(cv_h.at[:, :, cols], cv.at[g], sems.at[g, 4]),
            pltpu.make_async_copy(wo_h.at[cols, :], wo.at[g], sems.at[g, 5]),
        )

    @pl.when(i == 0)
    def _():
        for c in loads(0):
            c.start()

    @pl.when(i == SLOTS - 1)
    def _():
        for c in loads(1):
            c.start()

    @pl.when(i == 0)
    def _():
        pi = lax.broadcasted_iota(jnp.int32, (DRAFT, DRAFT), 0)
        qi = lax.broadcasted_iota(jnp.int32, (DRAFT, DRAFT), 1)
        eye = (qi == pi).astype(F32)
        who = lax.broadcasted_iota(jnp.int32, (DRAFT, 128), 1)
        lane = lax.broadcasted_iota(jnp.int32, (DRAFT, HD), 1)
        ones = jnp.ones((8, DRAFT), BF)
        ups = []
        for s in range(SLOTS):
            r = owner[base + s]
            par = jnp.sum(jnp.where(who == r, parents[...], 0), axis=1, keepdims=True)
            ups.append(jnp.where(par == qi, 1.0, eye))
        for rounds in range(6):
            nxt = []
            for up in ups:
                b = up.astype(BF)
                nxt.append(jnp.minimum(mm(b, b), 1.0))
            ups = nxt
        for s in range(SLOTS):
            r = owner[base + s]
            above = ups[s]
            above_s[s] = above
            depth_row = mm_nt(ones, above.astype(BF))[0:1] - 1.0
            depth = jnp.sum(above, axis=1, keepdims=True) - 1.0
            a = jnp.minimum(pick[r], dlen[r] - 1)
            path = above_s[s, pl.ds(a, 1), :]
            take = jnp.where(depth_row == pi.astype(F32), path, 0.0)
            take_s[s] = take.astype(BF)
            angle = (clen[r].astype(F32) + depth) * freq[...]
            at = slice(s * DRAFT, (s + 1) * DRAFT)
            cos_s[at, :] = jnp.cos(angle)
            sine = jnp.sin(angle)
            sin_s[at, :] = jnp.where(lane < HD // 2, -sine, sine)

    @pl.when(i < SLOTS)
    def _():
        s = i
        for p in range(DRAFT):
            raw[p * PITCH : p * PITCH + 64, :] = st[p * 64 : (p + 1) * 64, :].astype(F32)
        total = None
        for j in range(LT):
            x = hc_in[0, 0] * raw[pl.ds(j * NS, DRAFT, stride=PITCH), :]
            for m in range(1, NS):
                x = x + hc_in[0, m] * raw[pl.ds(j * NS + m, DRAFT, stride=PITCH), :]
            xbuf[:, j * 128 : (j + 1) * 128] = x
            total = x if total is None else total + x
        for j in range(LT):
            for n in range(NS):
                own[n, pl.ds(pl.multiple_of(s * Q, Q), Q), j * 128 : (j + 1) * 128] = raw[
                    pl.ds(place[1] * (Q * PITCH) + j * NS + n, Q, stride=PITCH), :
                ].astype(BF)
        center = jnp.sum(total, axis=-1, keepdims=True) * (1.0 / D)
        y = xbuf[...] - center
        spread = jnp.sum(y * y, axis=-1, keepdims=True) * (1.0 / D)
        normed[pl.ds(pl.multiple_of(s * DRAFT, DRAFT), DRAFT), :] = (
            y * lax.rsqrt(spread + 1e-05)
        ).astype(BF)

    def heads(g):
        arrive = loads(g)
        for c in arrive[:3]:
            c.wait()
        x = normed[...]
        q2 = mm(x, wq[g])
        k2 = mm(x, wk[g])
        v2 = mm(x, wv[g]).astype(BF)
        cosine = cos_s[...]
        sine = sin_s[...]
        col = lax.broadcasted_iota(jnp.int32, (DRAFT, CACHE), 1)
        for c in arrive[3:]:
            c.wait()
        kept = []
        for hh in range(2):
            cols = slice(hh * HD, (hh + 1) * HD)
            qh = q2[:, cols]
            kh = k2[:, cols]
            qh = (qh * cosine + pltpu.roll(qh, HD // 2, 1) * sine).astype(BF)
            kh = (kh * cosine + pltpu.roll(kh, HD // 2, 1) * sine).astype(BF)
            kept.append((cols, qh, kh, v2[:, cols]))
        todo = [(hh, s) for hh in range(2) for s in range(SLOTS)]
        for n, (hh, s) in enumerate(todo):
            cols, qh, kh, vh = kept[hh]
            at = slice(s * DRAFT, (s + 1) * DRAFT)
            to = slice(n * DRAFT, (n + 1) * DRAFT)
            length = clen[owner[base + s]]
            sc = mm_nt(qh[at], ck[g, s, :, cols]) * SCALE
            sc_s[to, :] = jnp.where(col < length, sc, -1e30)
            lo = mm_nt(qh[at], kh[at]) * SCALE
            lo_s[to, :] = jnp.where(above_s[s] > 0.5, lo, -1e30)
        for hh in range(2):
            to = slice(hh * 256, (hh + 1) * 256)
            sc = sc_s[to, :]
            lo = lo_s[to, :]
            top = jnp.maximum(
                jnp.max(sc, axis=-1, keepdims=True), jnp.max(lo, axis=-1, keepdims=True)
            )
            e1 = jnp.exp(sc - top)
            e2 = jnp.exp(lo - top)
            total = jnp.sum(e1, axis=-1, keepdims=True) + jnp.sum(e2, axis=-1, keepdims=True)
            inv = 1.0 / total
            w1_s[to, :] = (e1 * inv).astype(BF)
            w2_s[to, :] = (e2 * inv).astype(BF)
        for n, (hh, s) in enumerate(todo):
            cols, qh, kh, vh = kept[hh]
            at = slice(s * DRAFT, (s + 1) * DRAFT)
            to = slice(n * DRAFT, (n + 1) * DRAFT)
            o = mm(w1_s[to, :], cv[g, s, :, cols]) + mm(w2_s[to, :], vh[at])
            att[at, cols] = o.astype(BF)
            tk = take_s[s]
            h = g * 2 + hh
            kvs[s, pl.ds(h * 2, DRAFT, stride=8), :] = mm(tk, kh[at])
            kvs[s, pl.ds(h * 2 + 1, DRAFT, stride=8), :] = mm(tk, vh[at])
        part = mm(att[...], wo[g])
        if g == 0:
            acc[...] = part
        else:
            acc[...] = acc[...] + part
            for s in range(SLOTS):
                for k, out in enumerate((out0, out1, out2, out3)):
                    from_row = s * DRAFT + lax.rem(place[1] + k, 4) * Q
                    out[s * Q : (s + 1) * Q, :] = acc[
                        pl.ds(pl.multiple_of(from_row, Q), Q), :
                    ].astype(BF)
                kv_out[s * 512 : (s + 1) * 512, :] = kvs[s].astype(BF)

    @pl.when(i == SLOTS - 1)
    def _():
        heads(0)
        heads(1)


def front(place, owner, dlen, clen, pick, hc_in, parents, freq, st, wq, wk, wv, ck, cv, wo):
    smem = pl.BlockSpec(memory_space=pltpu.SMEM)
    vmem = pl.BlockSpec(memory_space=pltpu.VMEM)
    return pl.pallas_call(
        front_kernel,
        name="front",
        out_shape=(pltpu.VMEM((SLOTS * Q, D), BF),) * 4
        + (
            pltpu.VMEM((NS, SLOTS * Q, D), BF),
            jax.ShapeDtypeStruct((2048, 128), BF),
        ),
        grid_spec=pltpu.PrefetchScalarGridSpec(
            num_scalar_prefetch=5,
            grid=(SLOTS,),
            in_specs=[
                smem,
                pl.BlockSpec((DRAFT, 128), lambda i, *_: (0, 0)),
                pl.BlockSpec((1, HD), lambda i, *_: (0, 0)),
                pl.BlockSpec((4096, 128), lambda i, *_: (i, 0)),
            ]
            + [pl.BlockSpec(memory_space=pltpu.HBM)] * 6,
            out_specs=[vmem] * 5 + [pl.BlockSpec((2048, 128), lambda i, *_: (0, 0))],
            scratch_shapes=[
                pltpu.VMEM((DRAFT * PITCH, 128), F32),
                pltpu.VMEM((DRAFT, D), F32),
                pltpu.VMEM((SLOTS * DRAFT, D), BF),
                pltpu.VMEM((SLOTS, DRAFT, DRAFT), F32),
                pltpu.VMEM((SLOTS, DRAFT, DRAFT), BF),
                pltpu.VMEM((SLOTS * DRAFT, HD), F32),
                pltpu.VMEM((SLOTS * DRAFT, HD), F32),
                pltpu.VMEM((SLOTS * DRAFT, 256), BF),
                pltpu.VMEM((SLOTS * DRAFT, D), F32),
                pltpu.VMEM((SLOTS, 512, 128), F32),
                pltpu.VMEM((2, D, 256), BF),
                pltpu.VMEM((2, D, 256), BF),
                pltpu.VMEM((2, D, 256), BF),
                pltpu.VMEM((2, 256, D), BF),
                pltpu.VMEM((2, SLOTS, CACHE, 256), BF),
                pltpu.VMEM((2, SLOTS, CACHE, 256), BF),
                pltpu.VMEM((512, CACHE), F32),
                pltpu.VMEM((512, DRAFT), F32),
                pltpu.VMEM((512, CACHE), BF),
                pltpu.VMEM((512, DRAFT), BF),
                pltpu.SemaphoreType.DMA((2, 6)),
            ],
        ),
        compiler_params=pltpu.CompilerParams(vmem_limit_bytes=29 * 2**20),
    )(
        place,
        owner,
        dlen,
        clen,
        pick,
        hc_in,
        parents,
        freq,
        pltpu.with_memory_space_constraint(st, pltpu.HBM),
        *[pltpu.with_memory_space_constraint(x, pltpu.HBM) for x in (wq, wk, wv, wo, ck, cv)],
    )


def mid_kernel(hc_in, hc_res, hc_out, p0, p1, p2, p3, own, first, rows, xbuf):
    for s in range(SLOTS):
        at = slice(s * Q, (s + 1) * Q)
        total = None
        for j in range(LT):
            lanes = slice(j * 128, (j + 1) * 128)
            attn = p0[at, lanes].astype(F32)
            for p in (p1, p2, p3):
                attn = attn + p[at, lanes].astype(F32)
            mine = [own[n, at, lanes].astype(F32) for n in range(NS)]
            x = None
            for m in range(NS):
                c = hc_out[0, m] * attn
                for n in range(NS):
                    c = c + hc_res[0, n, m] * mine[n]
                c = c.astype(BF)
                first[m, at, lanes] = c
                t = hc_in[1, m] * c.astype(F32)
                x = t if x is None else x + t
            xbuf[at, lanes] = x
            total = x if total is None else total + x
        center = jnp.sum(total, axis=-1, keepdims=True) * (1.0 / D)
        y = xbuf[at, :] - center
        spread = jnp.sum(y * y, axis=-1, keepdims=True) * (1.0 / D)
        rows[at, :] = (y * lax.rsqrt(spread + 1e-05)).astype(BF)


def mid(hc_in, hc_res, hc_out, parts, own):
    smem = pl.BlockSpec(memory_space=pltpu.SMEM)
    vmem = pl.BlockSpec(memory_space=pltpu.VMEM)
    return pl.pallas_call(
        mid_kernel,
        name="mid",
        out_shape=(pltpu.VMEM((NS, SLOTS * Q, D), BF), pltpu.VMEM((SLOTS * Q, D), BF)),
        in_specs=[smem] * 3 + [vmem] * 5,
        out_specs=(vmem, vmem),
        scratch_shapes=[pltpu.VMEM((SLOTS * Q, D), F32)],
        compiler_params=pltpu.CompilerParams(vmem_limit_bytes=8 * 2**20),
    )(hc_in, hc_res, hc_out, *[near(p) for p in parts], near(own))


def last_kernel(place, owner, dlen, hc_res, hc_out, first, *refs):
    parts, out, raw = refs[:MEMBERS], refs[MEMBERS], refs[MEMBERS + 1]
    spot = place[1] * Q + lax.broadcasted_iota(jnp.int32, (Q, 128), 0)
    for s in range(SLOTS):
        at = slice(s * Q, (s + 1) * Q)
        alive = spot < dlen[owner[place[0] * SLOTS + s]]
        for j in range(LT):
            lanes = slice(j * 128, (j + 1) * 128)
            mlp = parts[0][at, lanes].astype(F32)
            for p in parts[1:]:
                mlp = mlp + p[at, lanes].astype(F32)
            f = [first[n, at, lanes].astype(F32) for n in range(NS)]
            for m in range(NS):
                c = hc_out[1, m] * mlp
                for n in range(NS):
                    c = c + hc_res[1, n, m] * f[n]
                raw[pl.ds(j * NS + m, Q, stride=PITCH), :] = jnp.where(alive, c, 0.0)
        for p in range(Q):
            out[(s * Q + p) * 64 : (s * Q + p + 1) * 64, :] = raw[
                p * PITCH : p * PITCH + 64, :
            ].astype(BF)


def last(place, owner, dlen, hc_res, hc_out, first, parts):
    smem = pl.BlockSpec(memory_space=pltpu.SMEM)
    vmem = pl.BlockSpec(memory_space=pltpu.VMEM)
    return pl.pallas_call(
        last_kernel,
        name="last",
        out_shape=jax.ShapeDtypeStruct((SLOTS * 1024, 128), BF),
        in_specs=[smem] * 5 + [vmem] * (1 + MEMBERS),
        out_specs=vmem,
        scratch_shapes=[pltpu.VMEM((Q * PITCH, 128), F32)],
        compiler_params=pltpu.CompilerParams(vmem_limit_bytes=8 * 2**20),
    )(place, owner, dlen, hc_res, hc_out, near(first), *[near(p) for p in parts])


def pack_kernel(g, u, d, one, two, sems):
    ins = []
    for k, w in enumerate((one, two)):
        part = pl.ds(k * 128, 128)
        ins.append(
            pltpu.make_async_copy(g.at[:, part], w.at[pl.ds(0, D), pl.ds(0, 128)], sems.at[k, 0])
        )
        ins.append(
            pltpu.make_async_copy(u.at[:, part], w.at[pl.ds(0, D), pl.ds(128, 128)], sems.at[k, 1])
        )
        for c in range(8):
            ins.append(
                pltpu.make_async_copy(
                    d.at[part, pl.ds(256 * c, 256)],
                    w.at[pl.ds(D + 128 * c, 128), :],
                    sems.at[k, 2 + c],
                )
            )
    for c in ins:
        c.start()
    for c in ins:
        c.wait()


def pack(g, u, d):
    hbm = pl.BlockSpec(memory_space=pltpu.HBM)
    vmem = pl.BlockSpec(memory_space=pltpu.VMEM)
    return pl.pallas_call(
        pack_kernel,
        name="pack",
        out_shape=(pltpu.VMEM((PACKED, 256), BF),) * 2,
        in_specs=[hbm] * 3,
        out_specs=(vmem, vmem),
        scratch_shapes=[pltpu.SemaphoreType.DMA((2, 10))],
        compiler_params=pltpu.CompilerParams(vmem_limit_bytes=8 * 2**20),
    )(*[pltpu.with_memory_space_constraint(x, pltpu.HBM) for x in (g, u, d)])


def ffn_kernel(n, *refs):
    xs, ws, ys = refs[:n], refs[n : n + BLOCKS], refs[n + BLOCKS : 2 * n + BLOCKS]
    cat, inner, wbuf, sems = refs[2 * n + BLOCKS :]
    copies = [pltpu.make_async_copy(ws[4 + k], wbuf.at[k], sems.at[k]) for k in range(4)]
    for c in copies:
        c.start()
    ws = list(ws[:4]) + [wbuf.at[k] for k in range(4)]
    rows = SLOTS * Q
    for k, x in enumerate(xs):
        cat[k * rows : (k + 1) * rows, :] = x[...]
    step = CH * rows
    spans = [(o, min(o + step, n * rows)) for o in range(0, n * rows, step)]
    for lo, hi in spans:
        for k, w in enumerate(ws):
            if k >= 4 and lo == 0:
                copies[k - 4].wait()
            both = mm(cat[lo:hi, :], w[:D, :])
            gate = both[:, :128]
            inner[lo:hi, k * 128 : (k + 1) * 128] = (
                gate / (1.0 + jnp.exp(-gate)) * both[:, 128:]
            ).astype(BF)
        for c in range(8):
            at = D + 128 * c
            down = jnp.concatenate([w[at : at + 128, :] for w in ws], axis=0)
            t = mm(inner[lo:hi, :], down).astype(BF)
            for k in range(lo // rows, hi // rows):
                ys[k][:, 256 * c : 256 * (c + 1)] = t[k * rows - lo : (k + 1) * rows - lo]


def ffn(xs, weights):
    n = len(xs)
    vmem = pl.BlockSpec(memory_space=pltpu.VMEM)
    rows = n * SLOTS * Q
    return pl.pallas_call(
        functools.partial(ffn_kernel, n),
        name="ffn",
        out_shape=tuple(pltpu.VMEM((SLOTS * Q, D), BF) for _ in xs),
        in_specs=[vmem] * (n + 4) + [pl.BlockSpec(memory_space=pltpu.HBM)] * 4,
        out_specs=tuple([vmem] * n),
        scratch_shapes=[
            pltpu.VMEM((rows, D), BF),
            pltpu.VMEM((rows, 128 * BLOCKS), BF),
            pltpu.VMEM((4, PACKED, 256), BF),
            pltpu.SemaphoreType.DMA((4,)),
        ],
        cost_estimate=pl.CostEstimate(
            flops=rows * D * 1024 * 6, transcendentals=rows * 1024, bytes_accessed=rows * D * 4
        ),
        compiler_params=pltpu.CompilerParams(vmem_limit_bytes=24 * 2**20),
    )(
        *[near(x) for x in list(xs) + list(weights[:4])],
        *[pltpu.with_memory_space_constraint(w, pltpu.HBM) for w in weights[4:]],
    )


def pairs(move):
    out = []
    for x in range(4):
        for z in range(4):
            for c in range(2):
                tx, tz, tc = move(x, z, c)
                out.append((x * 8 + z * 2 + c, (tx % 4) * 8 + (tz % 4) * 2 + tc))
    return out


def send(v, move):
    return lax.ppermute(v, "req", pairs(move))


def shift(v, dx, dz):
    return send(v, lambda x, z, c: (x + dx, z + dz, c))


def other_core(v):
    return send(v, lambda x, z, c: (x, z, 1 - c))


def body(
    streams,
    w_query,
    w_key,
    w_value,
    w_output,
    w_gate,
    w_up,
    w_down,
    cache_keys,
    cache_values,
    hc_in,
    hc_res,
    hc_out,
    parents,
    draft_len,
    cache_len,
    accept_pick,
    slot_owner,
):
    place = jnp.stack([lax.axis_index("req"), lax.axis_index("head")]).astype(jnp.int32)
    half = np.arange(64, dtype=np.float64)
    freq = np.power(10000.0, -(half * 2.0 / HD)).astype(np.float32)
    freq = jnp.asarray(np.concatenate([freq, freq])[None, :])
    st = streams.reshape(SLOTS, DRAFT, NS, LT, 128).transpose(0, 1, 3, 2, 4).reshape(-1, 128)
    one, two = pack(w_gate, w_up, w_down)
    one_z = send(one, lambda x, z, c: (x, z + 2 * c - 1, c))
    two_x = send(two, lambda x, z, c: (x + 2 * c - 1, z, c))
    one_c, two_c = other_core(one), other_core(two)
    *out, own, kv = front(
        place,
        slot_owner,
        draft_len,
        cache_len,
        accept_pick,
        hc_in,
        parents.T,
        freq,
        st,
        w_query,
        w_key,
        w_value,
        cache_keys,
        cache_values,
        w_output,
    )
    turn = lambda v, k: lax.ppermute(v, "head", [(y, (y + k) % 4) for y in range(4)])
    out, one_c, two_c, one_z, two_x = lax.optimization_barrier((out, one_c, two_c, one_z, two_x))
    one_zc, two_xc = other_core(one_z), other_core(two_x)
    p1 = turn(out[1], 1)
    p3 = turn(out[3], 3)
    p2 = turn(out[2], 2)
    weights = (one, two, one_zc, two_xc, one_c, two_c, one_z, two_x)
    first, rows = mid(hc_in, hc_res, hc_out, [out[0], p1, p2, p3], own)
    rows, weights = lax.optimization_barrier((rows, weights))
    pieces = [rows] + [shift(rows, dx, dz) for dx, dz in OFFSETS]
    sums = ffn(pieces[:FIRST], weights) + ffn(pieces[FIRST:], weights)
    back = [sums[0]] + [shift(t, -dx, -dz) for t, (dx, dz) in zip(sums[1:], OFFSETS)]
    final = last(place, slot_owner, draft_len, hc_res, hc_out, first, back)
    new_streams = (
        final.reshape(SLOTS, Q, LT, NS, 128).transpose(0, 1, 3, 2, 4).reshape(SLOTS, Q, NS, D)
    )
    accepted_kv = (
        kv.reshape(SLOTS, DRAFT, 4, 2, 128).transpose(0, 1, 3, 2, 4).reshape(SLOTS, DRAFT, 2, 512)
    )
    return (new_streams, accepted_kv)


def solution(mesh):
    placed = (
        P("req", None, None, None),
        P(None, "head"),
        P(None, "head"),
        P(None, "head"),
        P("head", None),
        P(None, "req"),
        P(None, "req"),
        P("req", None),
        P("req", None, "head"),
        P("req", None, "head"),
        P(),
        P(),
        P(),
        P(),
        P(),
        P(),
        P(),
        P(),
    )
    return jax.shard_map(
        body,
        mesh=mesh,
        in_specs=placed,
        out_specs=(P("req", "head", None, None), P("req", None, None, "head")),
        check_vma=False,
    )
```

```python
import functools

import jax
import jax.numpy as jnp
import numpy as np
from jax import lax
from jax.experimental import pallas as pl
from jax.experimental.pallas import tpu as pltpu
from jax.sharding import PartitionSpec as P

HD = 128
SLOTS = 4
DRAFT = 64
CACHE = 1024
D = 2048
NS = 4
LT = D // 128
Q = 16
SCALE = HD ** (-0.5)
BF = jnp.bfloat16
F32 = jnp.float32
BLOCKS = 8
PITCH = 72
PACKED = 3072
OFFSETS = ((1, 1), (-1, -1), (1, -1), (-1, 1), (2, 0), (0, 2), (2, 2))
MEMBERS = len(OFFSETS) + 1
CH = 4
NT = (((1,), (1,)), ((), ()))


def near(x):
    return pltpu.with_memory_space_constraint(x, pltpu.VMEM)


def mm(a, b):
    return jnp.dot(a, b, preferred_element_type=F32)


def mm_nt(a, b):
    return lax.dot_general(a, b, NT, preferred_element_type=F32)


def normalize(x):
    center = jnp.sum(x, axis=-1, keepdims=True) * (1.0 / D)
    y = x - center
    spread = jnp.sum(y * y, axis=-1, keepdims=True) * (1.0 / D)
    return y * lax.rsqrt(spread + 1e-05)


def front_kernel(
    place,
    owner,
    dlen,
    clen,
    pick,
    hc_in,
    parents,
    freq,
    st,
    wq_h,
    wk_h,
    wv_h,
    wo_h,
    ck_h,
    cv_h,
    out0,
    out1,
    out2,
    out3,
    own,
    kv_out,
    raw,
    xbuf,
    normed,
    above_s,
    take_s,
    cos_s,
    sin_s,
    att,
    acc,
    kvs,
    wq,
    wk,
    wv,
    wo,
    ck,
    cv,
    sc_s,
    lo_s,
    w1_s,
    w2_s,
    sems,
):
    i = pl.program_id(0)
    base = place[0] * SLOTS

    def loads(g):
        cols = pl.ds(g * 256, 256)
        return (
            pltpu.make_async_copy(wq_h.at[:, cols], wq.at[g], sems.at[g, 0]),
            pltpu.make_async_copy(wk_h.at[:, cols], wk.at[g], sems.at[g, 1]),
            pltpu.make_async_copy(wv_h.at[:, cols], wv.at[g], sems.at[g, 2]),
            pltpu.make_async_copy(ck_h.at[:, :, cols], ck.at[g], sems.at[g, 3]),
            pltpu.make_async_copy(cv_h.at[:, :, cols], cv.at[g], sems.at[g, 4]),
            pltpu.make_async_copy(wo_h.at[cols, :], wo.at[g], sems.at[g, 5]),
        )

    @pl.when(i == 0)
    def _():
        for c in loads(0):
            c.start()

    @pl.when(i == SLOTS - 1)
    def _():
        for c in loads(1):
            c.start()

    @pl.when(i == 0)
    def _():
        pi = lax.broadcasted_iota(jnp.int32, (DRAFT, DRAFT), 0)
        qi = lax.broadcasted_iota(jnp.int32, (DRAFT, DRAFT), 1)
        eye = (qi == pi).astype(F32)
        who = lax.broadcasted_iota(jnp.int32, (DRAFT, 128), 1)
        lane = lax.broadcasted_iota(jnp.int32, (DRAFT, HD), 1)
        ones = jnp.ones((8, DRAFT), BF)
        ups = []
        for s in range(SLOTS):
            r = owner[base + s]
            par = jnp.sum(jnp.where(who == r, parents[...], 0), axis=1, keepdims=True)
            ups.append(jnp.where(par == qi, 1.0, eye))
        for rounds in range(6):
            nxt = []
            for up in ups:
                b = up.astype(BF)
                nxt.append(jnp.minimum(mm(b, b), 1.0))
            ups = nxt
        for s in range(SLOTS):
            r = owner[base + s]
            above = ups[s]
            above_s[s] = above
            depth_row = mm_nt(ones, above.astype(BF))[0:1] - 1.0
            depth = jnp.sum(above, axis=1, keepdims=True) - 1.0
            a = jnp.minimum(pick[r], dlen[r] - 1)
            path = above_s[s, pl.ds(a, 1), :]
            take = jnp.where(depth_row == pi.astype(F32), path, 0.0)
            take_s[s] = take.astype(BF)
            angle = (clen[r].astype(F32) + depth) * freq[...]
            at = slice(s * DRAFT, (s + 1) * DRAFT)
            cos_s[at, :] = jnp.cos(angle)
            sine = jnp.sin(angle)
            sin_s[at, :] = jnp.where(lane < HD // 2, -sine, sine)

    @pl.when(i < SLOTS)
    def _():
        s = i
        for p in range(DRAFT):
            raw[p * PITCH : p * PITCH + 64, :] = st[p * 64 : (p + 1) * 64, :].astype(F32)
        total = None
        for j in range(LT):
            x = hc_in[0, 0] * raw[pl.ds(j * NS, DRAFT, stride=PITCH), :]
            for m in range(1, NS):
                x = x + hc_in[0, m] * raw[pl.ds(j * NS + m, DRAFT, stride=PITCH), :]
            xbuf[:, j * 128 : (j + 1) * 128] = x
            total = x if total is None else total + x
        for j in range(LT):
            for n in range(NS):
                own[n, pl.ds(pl.multiple_of(s * Q, Q), Q), j * 128 : (j + 1) * 128] = raw[
                    pl.ds(place[1] * (Q * PITCH) + j * NS + n, Q, stride=PITCH), :
                ].astype(BF)
        center = jnp.sum(total, axis=-1, keepdims=True) * (1.0 / D)
        y = xbuf[...] - center
        spread = jnp.sum(y * y, axis=-1, keepdims=True) * (1.0 / D)
        normed[pl.ds(pl.multiple_of(s * DRAFT, DRAFT), DRAFT), :] = (
            y * lax.rsqrt(spread + 1e-05)
        ).astype(BF)

    def heads(g):
        arrive = loads(g)
        for c in arrive[:3]:
            c.wait()
        x = normed[...]
        q2 = mm(x, wq[g])
        k2 = mm(x, wk[g])
        v2 = mm(x, wv[g]).astype(BF)
        cosine = cos_s[...]
        sine = sin_s[...]
        col = lax.broadcasted_iota(jnp.int32, (DRAFT, CACHE), 1)
        for c in arrive[3:]:
            c.wait()
        kept = []
        for hh in range(2):
            cols = slice(hh * HD, (hh + 1) * HD)
            qh = q2[:, cols]
            kh = k2[:, cols]
            qh = (qh * cosine + pltpu.roll(qh, HD // 2, 1) * sine).astype(BF)
            kh = (kh * cosine + pltpu.roll(kh, HD // 2, 1) * sine).astype(BF)
            kept.append((cols, qh, kh, v2[:, cols]))
        todo = [(hh, s) for hh in range(2) for s in range(SLOTS)]
        for n, (hh, s) in enumerate(todo):
            cols, qh, kh, vh = kept[hh]
            at = slice(s * DRAFT, (s + 1) * DRAFT)
            to = slice(n * DRAFT, (n + 1) * DRAFT)
            length = clen[owner[base + s]]
            sc = mm_nt(qh[at], ck[g, s, :, cols]) * SCALE
            sc_s[to, :] = jnp.where(col < length, sc, -1e30)
            lo = mm_nt(qh[at], kh[at]) * SCALE
            lo_s[to, :] = jnp.where(above_s[s] > 0.5, lo, -1e30)
        for hh in range(2):
            to = slice(hh * 256, (hh + 1) * 256)
            sc = sc_s[to, :]
            lo = lo_s[to, :]
            top = jnp.maximum(
                jnp.max(sc, axis=-1, keepdims=True), jnp.max(lo, axis=-1, keepdims=True)
            )
            e1 = jnp.exp(sc - top)
            e2 = jnp.exp(lo - top)
            total = jnp.sum(e1, axis=-1, keepdims=True) + jnp.sum(e2, axis=-1, keepdims=True)
            inv = 1.0 / total
            w1_s[to, :] = (e1 * inv).astype(BF)
            w2_s[to, :] = (e2 * inv).astype(BF)
        for n, (hh, s) in enumerate(todo):
            cols, qh, kh, vh = kept[hh]
            at = slice(s * DRAFT, (s + 1) * DRAFT)
            to = slice(n * DRAFT, (n + 1) * DRAFT)
            o = mm(w1_s[to, :], cv[g, s, :, cols]) + mm(w2_s[to, :], vh[at])
            att[at, cols] = o.astype(BF)
            tk = take_s[s]
            h = g * 2 + hh
            kvs[s, pl.ds(h * 2, DRAFT, stride=8), :] = mm(tk, kh[at])
            kvs[s, pl.ds(h * 2 + 1, DRAFT, stride=8), :] = mm(tk, vh[at])
        part = mm(att[...], wo[g])
        if g == 0:
            acc[...] = part
        else:
            acc[...] = acc[...] + part
            for s in range(SLOTS):
                for k, out in enumerate((out0, out1, out2, out3)):
                    from_row = s * DRAFT + lax.rem(place[1] + k, 4) * Q
                    out[s * Q : (s + 1) * Q, :] = acc[
                        pl.ds(pl.multiple_of(from_row, Q), Q), :
                    ].astype(BF)
                kv_out[s * 512 : (s + 1) * 512, :] = kvs[s].astype(BF)

    @pl.when(i == SLOTS - 1)
    def _():
        heads(0)
        heads(1)


def front(place, owner, dlen, clen, pick, hc_in, parents, freq, st, wq, wk, wv, ck, cv, wo):
    smem = pl.BlockSpec(memory_space=pltpu.SMEM)
    vmem = pl.BlockSpec(memory_space=pltpu.VMEM)
    return pl.pallas_call(
        front_kernel,
        name="front",
        out_shape=(pltpu.VMEM((SLOTS * Q, D), BF),) * 4
        + (
            pltpu.VMEM((NS, SLOTS * Q, D), BF),
            jax.ShapeDtypeStruct((2048, 128), BF),
        ),
        grid_spec=pltpu.PrefetchScalarGridSpec(
            num_scalar_prefetch=5,
            grid=(SLOTS,),
            in_specs=[
                smem,
                pl.BlockSpec((DRAFT, 128), lambda i, *_: (0, 0)),
                pl.BlockSpec((1, HD), lambda i, *_: (0, 0)),
                pl.BlockSpec((4096, 128), lambda i, *_: (i, 0)),
            ]
            + [pl.BlockSpec(memory_space=pltpu.HBM)] * 6,
            out_specs=[vmem] * 5 + [pl.BlockSpec((2048, 128), lambda i, *_: (0, 0))],
            scratch_shapes=[
                pltpu.VMEM((DRAFT * PITCH, 128), F32),
                pltpu.VMEM((DRAFT, D), F32),
                pltpu.VMEM((SLOTS * DRAFT, D), BF),
                pltpu.VMEM((SLOTS, DRAFT, DRAFT), F32),
                pltpu.VMEM((SLOTS, DRAFT, DRAFT), BF),
                pltpu.VMEM((SLOTS * DRAFT, HD), F32),
                pltpu.VMEM((SLOTS * DRAFT, HD), F32),
                pltpu.VMEM((SLOTS * DRAFT, 256), BF),
                pltpu.VMEM((SLOTS * DRAFT, D), F32),
                pltpu.VMEM((SLOTS, 512, 128), F32),
                pltpu.VMEM((2, D, 256), BF),
                pltpu.VMEM((2, D, 256), BF),
                pltpu.VMEM((2, D, 256), BF),
                pltpu.VMEM((2, 256, D), BF),
                pltpu.VMEM((2, SLOTS, CACHE, 256), BF),
                pltpu.VMEM((2, SLOTS, CACHE, 256), BF),
                pltpu.VMEM((512, CACHE), F32),
                pltpu.VMEM((512, DRAFT), F32),
                pltpu.VMEM((512, CACHE), BF),
                pltpu.VMEM((512, DRAFT), BF),
                pltpu.SemaphoreType.DMA((2, 6)),
            ],
        ),
        compiler_params=pltpu.CompilerParams(vmem_limit_bytes=29 * 2**20),
    )(
        place,
        owner,
        dlen,
        clen,
        pick,
        hc_in,
        parents,
        freq,
        pltpu.with_memory_space_constraint(st, pltpu.HBM),
        *[pltpu.with_memory_space_constraint(x, pltpu.HBM) for x in (wq, wk, wv, wo, ck, cv)],
    )


def mid_kernel(hc_in, hc_res, hc_out, p0, p1, p2, p3, own, first, rows, xbuf):
    for s in range(SLOTS):
        at = slice(s * Q, (s + 1) * Q)
        total = None
        for j in range(LT):
            lanes = slice(j * 128, (j + 1) * 128)
            attn = p0[at, lanes].astype(F32)
            for p in (p1, p2, p3):
                attn = attn + p[at, lanes].astype(F32)
            mine = [own[n, at, lanes].astype(F32) for n in range(NS)]
            x = None
            for m in range(NS):
                c = hc_out[0, m] * attn
                for n in range(NS):
                    c = c + hc_res[0, n, m] * mine[n]
                c = c.astype(BF)
                first[m, at, lanes] = c
                t = hc_in[1, m] * c.astype(F32)
                x = t if x is None else x + t
            xbuf[at, lanes] = x
            total = x if total is None else total + x
        center = jnp.sum(total, axis=-1, keepdims=True) * (1.0 / D)
        y = xbuf[at, :] - center
        spread = jnp.sum(y * y, axis=-1, keepdims=True) * (1.0 / D)
        rows[at, :] = (y * lax.rsqrt(spread + 1e-05)).astype(BF)


def mid(hc_in, hc_res, hc_out, parts, own):
    smem = pl.BlockSpec(memory_space=pltpu.SMEM)
    vmem = pl.BlockSpec(memory_space=pltpu.VMEM)
    return pl.pallas_call(
        mid_kernel,
        name="mid",
        out_shape=(pltpu.VMEM((NS, SLOTS * Q, D), BF), pltpu.VMEM((SLOTS * Q, D), BF)),
        in_specs=[smem] * 3 + [vmem] * 5,
        out_specs=(vmem, vmem),
        scratch_shapes=[pltpu.VMEM((SLOTS * Q, D), F32)],
        compiler_params=pltpu.CompilerParams(vmem_limit_bytes=8 * 2**20),
    )(hc_in, hc_res, hc_out, *[near(p) for p in parts], near(own))


def last_kernel(place, owner, dlen, hc_res, hc_out, first, *refs):
    parts, out, raw = refs[:MEMBERS], refs[MEMBERS], refs[MEMBERS + 1]
    spot = place[1] * Q + lax.broadcasted_iota(jnp.int32, (Q, 128), 0)
    for s in range(SLOTS):
        at = slice(s * Q, (s + 1) * Q)
        alive = spot < dlen[owner[place[0] * SLOTS + s]]
        for j in range(LT):
            lanes = slice(j * 128, (j + 1) * 128)
            mlp = parts[0][at, lanes].astype(F32)
            for p in parts[1:]:
                mlp = mlp + p[at, lanes].astype(F32)
            f = [first[n, at, lanes].astype(F32) for n in range(NS)]
            for m in range(NS):
                c = hc_out[1, m] * mlp
                for n in range(NS):
                    c = c + hc_res[1, n, m] * f[n]
                raw[pl.ds(j * NS + m, Q, stride=PITCH), :] = jnp.where(alive, c, 0.0)
        for p in range(Q):
            out[(s * Q + p) * 64 : (s * Q + p + 1) * 64, :] = raw[
                p * PITCH : p * PITCH + 64, :
            ].astype(BF)


def last(place, owner, dlen, hc_res, hc_out, first, parts):
    smem = pl.BlockSpec(memory_space=pltpu.SMEM)
    vmem = pl.BlockSpec(memory_space=pltpu.VMEM)
    return pl.pallas_call(
        last_kernel,
        name="last",
        out_shape=jax.ShapeDtypeStruct((SLOTS * 1024, 128), BF),
        in_specs=[smem] * 5 + [vmem] * (1 + MEMBERS),
        out_specs=vmem,
        scratch_shapes=[pltpu.VMEM((Q * PITCH, 128), F32)],
        compiler_params=pltpu.CompilerParams(vmem_limit_bytes=8 * 2**20),
    )(place, owner, dlen, hc_res, hc_out, near(first), *[near(p) for p in parts])


def pack_kernel(g, u, d, one, two, sems):
    ins = []
    for k, w in enumerate((one, two)):
        part = pl.ds(k * 128, 128)
        ins.append(
            pltpu.make_async_copy(g.at[:, part], w.at[pl.ds(0, D), pl.ds(0, 128)], sems.at[k, 0])
        )
        ins.append(
            pltpu.make_async_copy(u.at[:, part], w.at[pl.ds(0, D), pl.ds(128, 128)], sems.at[k, 1])
        )
        for c in range(8):
            ins.append(
                pltpu.make_async_copy(
                    d.at[part, pl.ds(256 * c, 256)],
                    w.at[pl.ds(D + 128 * c, 128), :],
                    sems.at[k, 2 + c],
                )
            )
    for c in ins:
        c.start()
    for c in ins:
        c.wait()


def pack(g, u, d):
    hbm = pl.BlockSpec(memory_space=pltpu.HBM)
    vmem = pl.BlockSpec(memory_space=pltpu.VMEM)
    return pl.pallas_call(
        pack_kernel,
        name="pack",
        out_shape=(pltpu.VMEM((PACKED, 256), BF),) * 2,
        in_specs=[hbm] * 3,
        out_specs=(vmem, vmem),
        scratch_shapes=[pltpu.SemaphoreType.DMA((2, 10))],
        compiler_params=pltpu.CompilerParams(vmem_limit_bytes=8 * 2**20),
    )(*[pltpu.with_memory_space_constraint(x, pltpu.HBM) for x in (g, u, d)])


def ffn_kernel(n, *refs):
    xs, ws, ys = refs[:n], refs[n : n + BLOCKS], refs[n + BLOCKS : 2 * n + BLOCKS]
    cat, inner, wbuf, sems = refs[2 * n + BLOCKS :]
    copies = [pltpu.make_async_copy(ws[4 + k], wbuf.at[k], sems.at[k]) for k in range(4)]
    for c in copies:
        c.start()
    ws = list(ws[:4]) + [wbuf.at[k] for k in range(4)]
    rows = SLOTS * Q
    for k, x in enumerate(xs):
        cat[k * rows : (k + 1) * rows, :] = x[...]
    step = CH * rows
    spans = [(o, min(o + step, n * rows)) for o in range(0, n * rows, step)]
    for lo, hi in spans:
        for k, w in enumerate(ws):
            if k >= 4 and lo == 0:
                copies[k - 4].wait()
            both = mm(cat[lo:hi, :], w[:D, :])
            gate = both[:, :128]
            inner[lo:hi, k * 128 : (k + 1) * 128] = (
                gate / (1.0 + jnp.exp(-gate)) * both[:, 128:]
            ).astype(BF)
        for c in range(8):
            at = D + 128 * c
            down = jnp.concatenate([w[at : at + 128, :] for w in ws], axis=0)
            t = mm(inner[lo:hi, :], down).astype(BF)
            for k in range(lo // rows, hi // rows):
                ys[k][:, 256 * c : 256 * (c + 1)] = t[k * rows - lo : (k + 1) * rows - lo]


def ffn(xs, weights):
    n = len(xs)
    vmem = pl.BlockSpec(memory_space=pltpu.VMEM)
    rows = n * SLOTS * Q
    return pl.pallas_call(
        functools.partial(ffn_kernel, n),
        name="ffn",
        out_shape=tuple(pltpu.VMEM((SLOTS * Q, D), BF) for _ in xs),
        in_specs=[vmem] * (n + 4) + [pl.BlockSpec(memory_space=pltpu.HBM)] * 4,
        out_specs=tuple([vmem] * n),
        scratch_shapes=[
            pltpu.VMEM((rows, D), BF),
            pltpu.VMEM((rows, 128 * BLOCKS), BF),
            pltpu.VMEM((4, PACKED, 256), BF),
            pltpu.SemaphoreType.DMA((4,)),
        ],
        cost_estimate=pl.CostEstimate(
            flops=rows * D * 1024 * 6, transcendentals=rows * 1024, bytes_accessed=rows * D * 4
        ),
        compiler_params=pltpu.CompilerParams(vmem_limit_bytes=24 * 2**20),
    )(
        *[near(x) for x in list(xs) + list(weights[:4])],
        *[pltpu.with_memory_space_constraint(w, pltpu.HBM) for w in weights[4:]],
    )


def pairs(move):
    out = []
    for x in range(4):
        for z in range(4):
            for c in range(2):
                tx, tz, tc = move(x, z, c)
                out.append((x * 8 + z * 2 + c, (tx % 4) * 8 + (tz % 4) * 2 + tc))
    return out


def send(v, move):
    return lax.ppermute(v, "req", pairs(move))


def shift(v, dx, dz):
    return send(v, lambda x, z, c: (x + dx, z + dz, c))


def other_core(v):
    return send(v, lambda x, z, c: (x, z, 1 - c))


def body(
    streams,
    w_query,
    w_key,
    w_value,
    w_output,
    w_gate,
    w_up,
    w_down,
    cache_keys,
    cache_values,
    hc_in,
    hc_res,
    hc_out,
    parents,
    draft_len,
    cache_len,
    accept_pick,
    slot_owner,
):
    place = jnp.stack([lax.axis_index("req"), lax.axis_index("head")]).astype(jnp.int32)
    half = np.arange(64, dtype=np.float64)
    freq = np.power(10000.0, -(half * 2.0 / HD)).astype(np.float32)
    freq = jnp.asarray(np.concatenate([freq, freq])[None, :])
    st = streams.reshape(SLOTS, DRAFT, NS, LT, 128).transpose(0, 1, 3, 2, 4).reshape(-1, 128)
    one, two = pack(w_gate, w_up, w_down)
    one_z = send(one, lambda x, z, c: (x, z + 2 * c - 1, c))
    two_x = send(two, lambda x, z, c: (x + 2 * c - 1, z, c))
    one_c, two_c = other_core(one), other_core(two)
    *out, own, kv = front(
        place,
        slot_owner,
        draft_len,
        cache_len,
        accept_pick,
        hc_in,
        parents.T,
        freq,
        st,
        w_query,
        w_key,
        w_value,
        cache_keys,
        cache_values,
        w_output,
    )
    turn = lambda v, k: lax.ppermute(v, "head", [(y, (y + k) % 4) for y in range(4)])
    out, one_c, two_c, one_z, two_x = lax.optimization_barrier((out, one_c, two_c, one_z, two_x))
    one_zc, two_xc = other_core(one_z), other_core(two_x)
    p1 = turn(out[1], 1)
    p3 = turn(out[3], 3)
    p2 = turn(out[2], 2)
    weights = (one, two, one_zc, two_xc, one_c, two_c, one_z, two_x)
    first, rows = mid(hc_in, hc_res, hc_out, [out[0], p1, p2, p3], own)
    rows, weights = lax.optimization_barrier((rows, weights))
    pieces = [rows] + [shift(rows, dx, dz) for dx, dz in OFFSETS]
    sums = ffn(pieces, weights)
    back = [sums[0]] + [shift(t, -dx, -dz) for t, (dx, dz) in zip(sums[1:], OFFSETS)]
    final = last(place, slot_owner, draft_len, hc_res, hc_out, first, back)
    new_streams = (
        final.reshape(SLOTS, Q, LT, NS, 128).transpose(0, 1, 3, 2, 4).reshape(SLOTS, Q, NS, D)
    )
    accepted_kv = (
        kv.reshape(SLOTS, DRAFT, 4, 2, 128).transpose(0, 1, 3, 2, 4).reshape(SLOTS, DRAFT, 2, 512)
    )
    return (new_streams, accepted_kv)


def solution(mesh):
    placed = (
        P("req", None, None, None),
        P(None, "head"),
        P(None, "head"),
        P(None, "head"),
        P("head", None),
        P(None, "req"),
        P(None, "req"),
        P("req", None),
        P("req", None, "head"),
        P("req", None, "head"),
        P(),
        P(),
        P(),
        P(),
        P(),
        P(),
        P(),
        P(),
    )
    return jax.shard_map(
        body,
        mesh=mesh,
        in_specs=placed,
        out_specs=(P("req", "head", None, None), P("req", None, None, "head")),
        check_vma=False,
    )
```

```python
import functools

import jax
import jax.numpy as jnp
import numpy as np
from jax import lax
from jax.experimental import pallas as pl
from jax.experimental.pallas import tpu as pltpu
from jax.sharding import PartitionSpec as P

HD = 128
SLOTS = 4
DRAFT = 64
CACHE = 1024
D = 2048
NS = 4
LT = D // 128
Q = 16
SCALE = HD ** (-0.5)
BF = jnp.bfloat16
F32 = jnp.float32
BLOCKS = 8
PITCH = 72
PACKED = 3072
OFFSETS = ((1, 1), (-1, -1), (1, -1), (-1, 1), (2, 0), (0, 2), (2, 2))
MEMBERS = len(OFFSETS) + 1
FIRST = 4
CH = 4
NT = (((1,), (1,)), ((), ()))


def near(x):
    return pltpu.with_memory_space_constraint(x, pltpu.VMEM)


def mm(a, b):
    return jnp.dot(a, b, preferred_element_type=F32)


def mm_nt(a, b):
    return lax.dot_general(a, b, NT, preferred_element_type=F32)


def normalize(x):
    center = jnp.sum(x, axis=-1, keepdims=True) * (1.0 / D)
    y = x - center
    spread = jnp.sum(y * y, axis=-1, keepdims=True) * (1.0 / D)
    return y * lax.rsqrt(spread + 1e-05)


def front_kernel(
    place,
    owner,
    dlen,
    clen,
    pick,
    hc_in,
    parents,
    freq,
    st,
    wq_h,
    wk_h,
    wv_h,
    wo_h,
    ck_h,
    cv_h,
    out0,
    out1,
    out2,
    out3,
    own,
    kv_out,
    raw,
    xbuf,
    normed,
    above_s,
    take_s,
    cos_s,
    sin_s,
    att,
    acc,
    kvs,
    wq,
    wk,
    wv,
    wo,
    ck,
    cv,
    sc_s,
    lo_s,
    w1_s,
    w2_s,
    sems,
):
    i = pl.program_id(0)
    base = place[0] * SLOTS

    def loads(g):
        cols = pl.ds(g * 256, 256)
        return (
            pltpu.make_async_copy(wq_h.at[:, cols], wq.at[g], sems.at[g, 0]),
            pltpu.make_async_copy(wk_h.at[:, cols], wk.at[g], sems.at[g, 1]),
            pltpu.make_async_copy(wv_h.at[:, cols], wv.at[g], sems.at[g, 2]),
            pltpu.make_async_copy(ck_h.at[:, :, cols], ck.at[g], sems.at[g, 3]),
            pltpu.make_async_copy(cv_h.at[:, :, cols], cv.at[g], sems.at[g, 4]),
            pltpu.make_async_copy(wo_h.at[cols, :], wo.at[g], sems.at[g, 5]),
        )

    @pl.when(i == 0)
    def _():
        for c in loads(0):
            c.start()

    @pl.when(i == SLOTS - 1)
    def _():
        for c in loads(1):
            c.start()

    @pl.when(i == 0)
    def _():
        pi = lax.broadcasted_iota(jnp.int32, (DRAFT, DRAFT), 0)
        qi = lax.broadcasted_iota(jnp.int32, (DRAFT, DRAFT), 1)
        eye = (qi == pi).astype(F32)
        who = lax.broadcasted_iota(jnp.int32, (DRAFT, 128), 1)
        lane = lax.broadcasted_iota(jnp.int32, (DRAFT, HD), 1)
        ones = jnp.ones((8, DRAFT), BF)
        ups = []
        for s in range(SLOTS):
            r = owner[base + s]
            par = jnp.sum(jnp.where(who == r, parents[...], 0), axis=1, keepdims=True)
            ups.append(jnp.where(par == qi, 1.0, eye))
        for rounds in range(6):
            nxt = []
            for up in ups:
                b = up.astype(BF)
                nxt.append(jnp.minimum(mm(b, b), 1.0))
            ups = nxt
        for s in range(SLOTS):
            r = owner[base + s]
            above = ups[s]
            above_s[s] = above
            depth_row = mm_nt(ones, above.astype(BF))[0:1] - 1.0
            depth = jnp.sum(above, axis=1, keepdims=True) - 1.0
            a = jnp.minimum(pick[r], dlen[r] - 1)
            path = above_s[s, pl.ds(a, 1), :]
            take = jnp.where(depth_row == pi.astype(F32), path, 0.0)
            take_s[s] = take.astype(BF)
            angle = (clen[r].astype(F32) + depth) * freq[...]
            at = slice(s * DRAFT, (s + 1) * DRAFT)
            cos_s[at, :] = jnp.cos(angle)
            sine = jnp.sin(angle)
            sin_s[at, :] = jnp.where(lane < HD // 2, -sine, sine)

    @pl.when(i < SLOTS)
    def _():
        s = i
        for p in range(DRAFT):
            raw[p * PITCH : p * PITCH + 64, :] = st[p * 64 : (p + 1) * 64, :].astype(F32)
        total = None
        for j in range(LT):
            x = hc_in[0, 0] * raw[pl.ds(j * NS, DRAFT, stride=PITCH), :]
            for m in range(1, NS):
                x = x + hc_in[0, m] * raw[pl.ds(j * NS + m, DRAFT, stride=PITCH), :]
            xbuf[:, j * 128 : (j + 1) * 128] = x
            total = x if total is None else total + x
        for j in range(LT):
            for n in range(NS):
                own[n, pl.ds(pl.multiple_of(s * Q, Q), Q), j * 128 : (j + 1) * 128] = raw[
                    pl.ds(place[1] * (Q * PITCH) + j * NS + n, Q, stride=PITCH), :
                ].astype(BF)
        center = jnp.sum(total, axis=-1, keepdims=True) * (1.0 / D)
        y = xbuf[...] - center
        spread = jnp.sum(y * y, axis=-1, keepdims=True) * (1.0 / D)
        normed[pl.ds(pl.multiple_of(s * DRAFT, DRAFT), DRAFT), :] = (
            y * lax.rsqrt(spread + 1e-05)
        ).astype(BF)

    def heads(g):
        arrive = loads(g)
        for c in arrive[:3]:
            c.wait()
        x = normed[...]
        q2 = mm(x, wq[g])
        k2 = mm(x, wk[g])
        v2 = mm(x, wv[g]).astype(BF)
        cosine = cos_s[...]
        sine = sin_s[...]
        col = lax.broadcasted_iota(jnp.int32, (DRAFT, CACHE), 1)
        for c in arrive[3:]:
            c.wait()
        kept = []
        for hh in range(2):
            cols = slice(hh * HD, (hh + 1) * HD)
            qh = q2[:, cols]
            kh = k2[:, cols]
            qh = (qh * cosine + pltpu.roll(qh, HD // 2, 1) * sine).astype(BF)
            kh = (kh * cosine + pltpu.roll(kh, HD // 2, 1) * sine).astype(BF)
            kept.append((cols, qh, kh, v2[:, cols]))
        todo = [(hh, s) for hh in range(2) for s in range(SLOTS)]
        for n, (hh, s) in enumerate(todo):
            cols, qh, kh, vh = kept[hh]
            at = slice(s * DRAFT, (s + 1) * DRAFT)
            to = slice(n * DRAFT, (n + 1) * DRAFT)
            length = clen[owner[base + s]]
            sc = mm_nt(qh[at], ck[g, s, :, cols]) * SCALE
            sc_s[to, :] = jnp.where(col < length, sc, -1e30)
            lo = mm_nt(qh[at], kh[at]) * SCALE
            lo_s[to, :] = jnp.where(above_s[s] > 0.5, lo, -1e30)
        for hh in range(2):
            to = slice(hh * 256, (hh + 1) * 256)
            sc = sc_s[to, :]
            lo = lo_s[to, :]
            top = jnp.maximum(
                jnp.max(sc, axis=-1, keepdims=True), jnp.max(lo, axis=-1, keepdims=True)
            )
            e1 = jnp.exp(sc - top)
            e2 = jnp.exp(lo - top)
            total = jnp.sum(e1, axis=-1, keepdims=True) + jnp.sum(e2, axis=-1, keepdims=True)
            inv = 1.0 / total
            w1_s[to, :] = (e1 * inv).astype(BF)
            w2_s[to, :] = (e2 * inv).astype(BF)
        for n, (hh, s) in enumerate(todo):
            cols, qh, kh, vh = kept[hh]
            at = slice(s * DRAFT, (s + 1) * DRAFT)
            to = slice(n * DRAFT, (n + 1) * DRAFT)
            o = mm(w1_s[to, :], cv[g, s, :, cols]) + mm(w2_s[to, :], vh[at])
            att[at, cols] = o.astype(BF)
            tk = take_s[s]
            h = g * 2 + hh
            kvs[s, pl.ds(h * 2, DRAFT, stride=8), :] = mm(tk, kh[at])
            kvs[s, pl.ds(h * 2 + 1, DRAFT, stride=8), :] = mm(tk, vh[at])
        part = mm(att[...], wo[g])
        if g == 0:
            acc[...] = part
        else:
            acc[...] = acc[...] + part
            for s in range(SLOTS):
                for k, out in enumerate((out0, out1, out2, out3)):
                    from_row = s * DRAFT + lax.rem(place[1] + k, 4) * Q
                    out[s * Q : (s + 1) * Q, :] = acc[
                        pl.ds(pl.multiple_of(from_row, Q), Q), :
                    ].astype(BF)
                kv_out[s * 512 : (s + 1) * 512, :] = kvs[s].astype(BF)

    @pl.when(i == SLOTS - 1)
    def _():
        heads(0)
        heads(1)


def front(place, owner, dlen, clen, pick, hc_in, parents, freq, st, wq, wk, wv, ck, cv, wo):
    smem = pl.BlockSpec(memory_space=pltpu.SMEM)
    vmem = pl.BlockSpec(memory_space=pltpu.VMEM)
    return pl.pallas_call(
        front_kernel,
        name="front",
        out_shape=(pltpu.VMEM((SLOTS * Q, D), BF),) * 4
        + (
            pltpu.VMEM((NS, SLOTS * Q, D), BF),
            jax.ShapeDtypeStruct((2048, 128), BF),
        ),
        grid_spec=pltpu.PrefetchScalarGridSpec(
            num_scalar_prefetch=5,
            grid=(SLOTS,),
            in_specs=[
                smem,
                pl.BlockSpec((DRAFT, 128), lambda i, *_: (0, 0)),
                pl.BlockSpec((1, HD), lambda i, *_: (0, 0)),
                pl.BlockSpec((4096, 128), lambda i, *_: (i, 0)),
            ]
            + [pl.BlockSpec(memory_space=pltpu.HBM)] * 6,
            out_specs=[vmem] * 5 + [pl.BlockSpec((2048, 128), lambda i, *_: (0, 0))],
            scratch_shapes=[
                pltpu.VMEM((DRAFT * PITCH, 128), F32),
                pltpu.VMEM((DRAFT, D), F32),
                pltpu.VMEM((SLOTS * DRAFT, D), BF),
                pltpu.VMEM((SLOTS, DRAFT, DRAFT), F32),
                pltpu.VMEM((SLOTS, DRAFT, DRAFT), BF),
                pltpu.VMEM((SLOTS * DRAFT, HD), F32),
                pltpu.VMEM((SLOTS * DRAFT, HD), F32),
                pltpu.VMEM((SLOTS * DRAFT, 256), BF),
                pltpu.VMEM((SLOTS * DRAFT, D), F32),
                pltpu.VMEM((SLOTS, 512, 128), F32),
                pltpu.VMEM((2, D, 256), BF),
                pltpu.VMEM((2, D, 256), BF),
                pltpu.VMEM((2, D, 256), BF),
                pltpu.VMEM((2, 256, D), BF),
                pltpu.VMEM((2, SLOTS, CACHE, 256), BF),
                pltpu.VMEM((2, SLOTS, CACHE, 256), BF),
                pltpu.VMEM((512, CACHE), F32),
                pltpu.VMEM((512, DRAFT), F32),
                pltpu.VMEM((512, CACHE), BF),
                pltpu.VMEM((512, DRAFT), BF),
                pltpu.SemaphoreType.DMA((2, 6)),
            ],
        ),
        compiler_params=pltpu.CompilerParams(vmem_limit_bytes=29 * 2**20),
    )(
        place,
        owner,
        dlen,
        clen,
        pick,
        hc_in,
        parents,
        freq,
        pltpu.with_memory_space_constraint(st, pltpu.HBM),
        *[pltpu.with_memory_space_constraint(x, pltpu.HBM) for x in (wq, wk, wv, wo, ck, cv)],
    )


def mid_kernel(hc_in, hc_res, hc_out, p0, p1, p2, p3, own, first, rows, xbuf):
    for s in range(SLOTS):
        at = slice(s * Q, (s + 1) * Q)
        total = None
        for j in range(LT):
            lanes = slice(j * 128, (j + 1) * 128)
            attn = p0[at, lanes].astype(F32)
            for p in (p1, p2, p3):
                attn = attn + p[at, lanes].astype(F32)
            mine = [own[n, at, lanes].astype(F32) for n in range(NS)]
            x = None
            for m in range(NS):
                c = hc_out[0, m] * attn
                for n in range(NS):
                    c = c + hc_res[0, n, m] * mine[n]
                c = c.astype(BF)
                first[m, at, lanes] = c
                t = hc_in[1, m] * c.astype(F32)
                x = t if x is None else x + t
            xbuf[at, lanes] = x
            total = x if total is None else total + x
        center = jnp.sum(total, axis=-1, keepdims=True) * (1.0 / D)
        y = xbuf[at, :] - center
        spread = jnp.sum(y * y, axis=-1, keepdims=True) * (1.0 / D)
        rows[at, :] = (y * lax.rsqrt(spread + 1e-05)).astype(BF)


def mid(hc_in, hc_res, hc_out, parts, own):
    smem = pl.BlockSpec(memory_space=pltpu.SMEM)
    vmem = pl.BlockSpec(memory_space=pltpu.VMEM)
    return pl.pallas_call(
        mid_kernel,
        name="mid",
        out_shape=(pltpu.VMEM((NS, SLOTS * Q, D), BF), pltpu.VMEM((SLOTS * Q, D), BF)),
        in_specs=[smem] * 3 + [vmem] * 5,
        out_specs=(vmem, vmem),
        scratch_shapes=[pltpu.VMEM((SLOTS * Q, D), F32)],
        compiler_params=pltpu.CompilerParams(vmem_limit_bytes=8 * 2**20),
    )(hc_in, hc_res, hc_out, *[near(p) for p in parts], near(own))


def last_kernel(place, owner, dlen, hc_res, hc_out, first, *refs):
    parts, out, raw = refs[:MEMBERS], refs[MEMBERS], refs[MEMBERS + 1]
    spot = place[1] * Q + lax.broadcasted_iota(jnp.int32, (Q, 128), 0)
    for s in range(SLOTS):
        at = slice(s * Q, (s + 1) * Q)
        alive = spot < dlen[owner[place[0] * SLOTS + s]]
        for j in range(LT):
            lanes = slice(j * 128, (j + 1) * 128)
            mlp = parts[0][at, lanes].astype(F32)
            for p in parts[1:]:
                mlp = mlp + p[at, lanes].astype(F32)
            f = [first[n, at, lanes].astype(F32) for n in range(NS)]
            for m in range(NS):
                c = hc_out[1, m] * mlp
                for n in range(NS):
                    c = c + hc_res[1, n, m] * f[n]
                raw[pl.ds(j * NS + m, Q, stride=PITCH), :] = jnp.where(alive, c, 0.0)
        for p in range(Q):
            out[(s * Q + p) * 64 : (s * Q + p + 1) * 64, :] = raw[
                p * PITCH : p * PITCH + 64, :
            ].astype(BF)


def last(place, owner, dlen, hc_res, hc_out, first, parts):
    smem = pl.BlockSpec(memory_space=pltpu.SMEM)
    vmem = pl.BlockSpec(memory_space=pltpu.VMEM)
    return pl.pallas_call(
        last_kernel,
        name="last",
        out_shape=jax.ShapeDtypeStruct((SLOTS * 1024, 128), BF),
        in_specs=[smem] * 5 + [vmem] * (1 + MEMBERS),
        out_specs=vmem,
        scratch_shapes=[pltpu.VMEM((Q * PITCH, 128), F32)],
        compiler_params=pltpu.CompilerParams(vmem_limit_bytes=8 * 2**20),
    )(place, owner, dlen, hc_res, hc_out, near(first), *[near(p) for p in parts])


def pack_kernel(g, u, d, one, two, sems):
    ins = []
    for k, w in enumerate((one, two)):
        part = pl.ds(k * 128, 128)
        ins.append(
            pltpu.make_async_copy(g.at[:, part], w.at[pl.ds(0, D), pl.ds(0, 128)], sems.at[k, 0])
        )
        ins.append(
            pltpu.make_async_copy(u.at[:, part], w.at[pl.ds(0, D), pl.ds(128, 128)], sems.at[k, 1])
        )
        for c in range(8):
            ins.append(
                pltpu.make_async_copy(
                    d.at[part, pl.ds(256 * c, 256)],
                    w.at[pl.ds(D + 128 * c, 128), :],
                    sems.at[k, 2 + c],
                )
            )
    for c in ins:
        c.start()
    for c in ins:
        c.wait()


def pack(g, u, d):
    hbm = pl.BlockSpec(memory_space=pltpu.HBM)
    vmem = pl.BlockSpec(memory_space=pltpu.VMEM)
    return pl.pallas_call(
        pack_kernel,
        name="pack",
        out_shape=(pltpu.VMEM((PACKED, 256), BF),) * 2,
        in_specs=[hbm] * 3,
        out_specs=(vmem, vmem),
        scratch_shapes=[pltpu.SemaphoreType.DMA((2, 10))],
        compiler_params=pltpu.CompilerParams(vmem_limit_bytes=8 * 2**20),
    )(*[pltpu.with_memory_space_constraint(x, pltpu.HBM) for x in (g, u, d)])


def ffn_kernel(n, *refs):
    xs, ws, ys = refs[:n], refs[n : n + BLOCKS], refs[n + BLOCKS : 2 * n + BLOCKS]
    cat, inner, wbuf, sems = refs[2 * n + BLOCKS :]
    copies = [pltpu.make_async_copy(ws[4 + k], wbuf.at[k], sems.at[k]) for k in range(4)]
    for c in copies:
        c.start()
    ws = list(ws[:4]) + [wbuf.at[k] for k in range(4)]
    rows = SLOTS * Q
    for k, x in enumerate(xs):
        cat[k * rows : (k + 1) * rows, :] = x[...]
    step = CH * rows
    spans = [(o, min(o + step, n * rows)) for o in range(0, n * rows, step)]
    for lo, hi in spans:
        for k, w in enumerate(ws):
            if k >= 4 and lo == 0:
                copies[k - 4].wait()
            both = mm(cat[lo:hi, :], w[:D, :])
            gate = both[:, :128]
            inner[lo:hi, k * 128 : (k + 1) * 128] = (
                gate / (1.0 + jnp.exp(-gate)) * both[:, 128:]
            ).astype(BF)
        for c in range(8):
            at = D + 128 * c
            down = jnp.concatenate([w[at : at + 128, :] for w in ws], axis=0)
            t = mm(inner[lo:hi, :], down).astype(BF)
            for k in range(lo // rows, hi // rows):
                ys[k][:, 256 * c : 256 * (c + 1)] = t[k * rows - lo : (k + 1) * rows - lo]


def ffn(xs, weights):
    n = len(xs)
    vmem = pl.BlockSpec(memory_space=pltpu.VMEM)
    rows = n * SLOTS * Q
    return pl.pallas_call(
        functools.partial(ffn_kernel, n),
        name="ffn",
        out_shape=tuple(pltpu.VMEM((SLOTS * Q, D), BF) for _ in xs),
        in_specs=[vmem] * (n + 4) + [pl.BlockSpec(memory_space=pltpu.HBM)] * 4,
        out_specs=tuple([vmem] * n),
        scratch_shapes=[
            pltpu.VMEM((rows, D), BF),
            pltpu.VMEM((rows, 128 * BLOCKS), BF),
            pltpu.VMEM((4, PACKED, 256), BF),
            pltpu.SemaphoreType.DMA((4,)),
        ],
        cost_estimate=pl.CostEstimate(
            flops=rows * D * 1024 * 6, transcendentals=rows * 1024, bytes_accessed=rows * D * 4
        ),
        compiler_params=pltpu.CompilerParams(vmem_limit_bytes=24 * 2**20),
    )(
        *[near(x) for x in list(xs) + list(weights[:4])],
        *[pltpu.with_memory_space_constraint(w, pltpu.HBM) for w in weights[4:]],
    )


def pairs(move):
    out = []
    for x in range(4):
        for z in range(4):
            for c in range(2):
                tx, tz, tc = move(x, z, c)
                out.append((x * 8 + z * 2 + c, (tx % 4) * 8 + (tz % 4) * 2 + tc))
    return out


def send(v, move):
    return lax.ppermute(v, "req", pairs(move))


def shift(v, dx, dz):
    return send(v, lambda x, z, c: (x + dx, z + dz, c))


def other_core(v):
    return send(v, lambda x, z, c: (x, z, 1 - c))


def body(
    streams,
    w_query,
    w_key,
    w_value,
    w_output,
    w_gate,
    w_up,
    w_down,
    cache_keys,
    cache_values,
    hc_in,
    hc_res,
    hc_out,
    parents,
    draft_len,
    cache_len,
    accept_pick,
    slot_owner,
):
    place = jnp.stack([lax.axis_index("req"), lax.axis_index("head")]).astype(jnp.int32)
    half = np.arange(64, dtype=np.float64)
    freq = np.power(10000.0, -(half * 2.0 / HD)).astype(np.float32)
    freq = jnp.asarray(np.concatenate([freq, freq])[None, :])
    st = streams.reshape(SLOTS, DRAFT, NS, LT, 128).transpose(0, 1, 3, 2, 4).reshape(-1, 128)
    one, two = pack(w_gate, w_up, w_down)
    one_z = send(one, lambda x, z, c: (x, z ^ 1, c))
    two_x = send(two, lambda x, z, c: (x ^ 1, z, c))
    one_c, two_c = other_core(one), other_core(two)
    *out, own, kv = front(
        place,
        slot_owner,
        draft_len,
        cache_len,
        accept_pick,
        hc_in,
        parents.T,
        freq,
        st,
        w_query,
        w_key,
        w_value,
        cache_keys,
        cache_values,
        w_output,
    )
    turn = lambda v, k: lax.ppermute(v, "head", [(y, (y + k) % 4) for y in range(4)])
    out, one_c, two_c = lax.optimization_barrier((out, one_c, two_c))
    p1 = turn(out[1], 1)
    p3 = turn(out[3], 3)
    p2 = turn(out[2], 2)
    p1, p2, p3, one_z, two_x = lax.optimization_barrier((p1, p2, p3, one_z, two_x))
    weights = (one, two, other_core(one_z), other_core(two_x), one_c, two_c, one_z, two_x)
    first, rows = mid(hc_in, hc_res, hc_out, [out[0], p1, p2, p3], own)
    rows, weights = lax.optimization_barrier((rows, weights))
    pieces = [rows] + [shift(rows, dx, dz) for dx, dz in OFFSETS]
    sums = ffn(pieces, weights)
    back = [sums[0]] + [shift(t, -dx, -dz) for t, (dx, dz) in zip(sums[1:], OFFSETS)]
    final = last(place, slot_owner, draft_len, hc_res, hc_out, first, back)
    new_streams = (
        final.reshape(SLOTS, Q, LT, NS, 128).transpose(0, 1, 3, 2, 4).reshape(SLOTS, Q, NS, D)
    )
    accepted_kv = (
        kv.reshape(SLOTS, DRAFT, 4, 2, 128).transpose(0, 1, 3, 2, 4).reshape(SLOTS, DRAFT, 2, 512)
    )
    return (new_streams, accepted_kv)


def solution(mesh):
    placed = (
        P("req", None, None, None),
        P(None, "head"),
        P(None, "head"),
        P(None, "head"),
        P("head", None),
        P(None, "req"),
        P(None, "req"),
        P("req", None),
        P("req", None, "head"),
        P("req", None, "head"),
        P(),
        P(),
        P(),
        P(),
        P(),
        P(),
        P(),
        P(),
    )
    return jax.shard_map(
        body,
        mesh=mesh,
        in_specs=placed,
        out_specs=(P("req", "head", None, None), P("req", None, None, "head")),
        check_vma=False,
    )
```
